256 devices in a mesh: expert: 32 (over x, y, core), shard: 8 (over z).
Axes of the slice: x: 4, y: 4, z: 8, core: 2. Of those that a mesh axis runs over, the one named last changes fastest.
Arguments:
- head_outputs: bfloat16 [32768, 1024], P(('expert', 'shard')), may hold values from -6 to 6
- residual: bfloat16 [32768, 1024], P(('expert', 'shard')), may hold values from -4 to 4
- output_weight: bfloat16 [1024, 1024], P('shard'), may hold values from -0.1875 to 0.1875
- router: bfloat16 [1024, 32], replicated, may hold values from -0.095703125 to 0.095703125
- norm_gain: float32 [1024], replicated, may hold values from 0.1 to 1.9
- placed_gate_up: bfloat16 [64, 1024, 1024], P('expert', 'shard'), may hold values from -0.1875 to 0.1875
- placed_down: bfloat16 [64, 512, 1024], P('expert', 'shard'), may hold values from -0.25 to 0.25
- routes: int32 [32768, 8], P(('expert', 'shard')), may hold values from 0 to 31, all different within a row; in each aligned block of 128 rows (0 to 127, 128 to 255, ...) at most 48 rows name the same one
- replica_pick: int32 [32768, 8], P(('expert', 'shard')), may hold values from 0 to 5
- placement: int32 [64], replicated, may hold values from 0 to 31, as said below
- final_gain: float32 [1024], replicated, may hold values from 0.1 to 1.9
Outputs:
- next_input: bfloat16 [32768, 1024], P(('expert', 'shard'))
The draws below stay inside these ranges and needn't reach their ends.
Inputs may be any that keep to these rules, and one draw needn't show every extreme that they name: `routes`: each token names 8 different experts. Among the 128 tokens of one device no expert is named more than 48 times, and in some device's tokens one expert is named exactly 48 times. `placement`: every expert holds one to three of the 64 placements: a quarter of the experts hold three, half of them two, the rest one.
All inputs are finite; a program needn't handle non-finite values.
Results may differ from the reference program's by a relative error of at most 0.011.
Values may be sent and summed in bfloat16 or wider, within the bound.
A program may use at most 128 MiB of HBM per device.

```python
import math
import jax
import jax.numpy as jnp
import numpy as np
from jax import lax

D = 1024
FF = 512
EXPERTS = 32
TOP = 8
TOK_DEV = 128
CAP = 48
PL = 64
TOKENS = 32768


def draw_placement(key, part):
    shuffled = jax.random.permutation(jax.random.fold_in(key, 11), EXPERTS).astype(jnp.int32)
    quarter = EXPERTS // 4
    half_count = EXPERTS // 2
    copies = np.array([3] * quarter + [2] * half_count + [1] * (EXPERTS - quarter - half_count))
    listed = jnp.repeat(shuffled, copies, total_repeat_length=PL)
    return jax.random.permutation(jax.random.fold_in(key, 12), listed).astype(jnp.int32)


def plant(values, rng, least, high):
    extent = values.shape
    index_at = [jax.random.randint(jax.random.fold_in(rng, axis), (), 0, extent[axis]) for axis in range(len(extent))]
    values = values.at[tuple(index_at)].set(least)
    longest = extent.index(max(extent))
    index_at[longest] = (index_at[longest] + 1) % extent[longest]
    return values.at[tuple(index_at)].set(high)


def block_scale(stream_key, dims, split, least, high):
    def one(dim, parts):
        heights = jax.random.uniform(jax.random.fold_in(jax.random.fold_in(stream_key, 6), dim), (parts,), jnp.float32, least / len(split), high / len(split))
        return jnp.repeat(jnp.exp(heights), dims[dim] // parts).reshape((-1,) + (1,) * (len(dims) - dim - 1))

    gain = one(*split[0])
    for cut in split[1:]:
        gain = gain * one(*cut)
    return gain


def deal_out(key, own, number, rows, amount, top, reach, skew):
    order = jax.random.permutation(key, amount)
    packed, usual = portions_of(amount, rows * top, reach, skew, True), portions_of(amount, rows * top, reach, skew, False)
    places = jnp.arange(amount)

    def named(sizes, rotation):
        used = int((sizes > 0).sum())
        fixed = max(1, used // 4)
        moved = fixed + (places - fixed + rotation * (used - fixed)) % max(1, amount - fixed)
        return jnp.zeros((amount,), jnp.int32).at[order[jnp.where(places < fixed, places, moved)]].set(jnp.asarray(sizes, jnp.int32))

    sizes = jnp.where(number % 4 == 0, named(packed, number // 4), named(usual, number - number // 4 - 1))
    mixed = jax.random.permutation(jax.random.fold_in(own, 3), amount)
    giver, sink = mixed[0:amount // 2 * 2:2], mixed[1:amount // 2 * 2:2]
    room = jnp.minimum(sizes[giver] - 1, reach - sizes[sink]) // 2
    room = jnp.where((giver == order[0]) | (sink == order[0]) | (sizes[sink] == 0), 0, jnp.maximum(room, 0))
    moved = jax.random.randint(jax.random.fold_in(own, 4), (amount // 2,), 0, 1 << 20) % (room + 1)
    sizes = sizes.at[giver].add(-moved).at[sink].add(moved)
    items = jnp.searchsorted(jnp.cumsum(sizes), jnp.arange(rows * top), side="right").astype(jnp.int32)
    table = items.reshape(top, rows).T
    table = table[jax.random.permutation(jax.random.fold_in(own, 1), rows)]
    rotation = jax.random.randint(jax.random.fold_in(own, 2), (rows, 1), 0, top)
    return jnp.take_along_axis(table, (jnp.arange(top)[None, :] + rotation) % top, axis=1)


def portions_of(number_of, total, bound, lean, full):
    loads = [(1 << 20) // math.isqrt(standing ** lean) + 1 for standing in range(1, number_of + 1)]
    largest = bound if full else min(bound, max(-(-total // number_of), total * loads[0] // sum(loads)))
    least = 1 if total - largest >= number_of - 1 else 0
    given, spare = [largest] + [least] * (number_of - 1), total - largest - least * (number_of - 1)
    while spare > 0:
        candidates = [i for i in range(1, number_of) if given[i] < largest] or [i for i in range(1, number_of) if given[i] < bound]
        mass, remaining = sum([loads[i] for i in candidates]), spare
        for i in candidates:
            extra = min(bound - given[i], max(1, remaining * loads[i] // mass), spare)
            given[i] = given[i] + extra
            spare = spare - extra
    return np.array(given)


def bell_draw(stream_key, shape, width, most, shards=(), kind=jnp.bfloat16):
    values = width * jax.random.normal(stream_key, shape, jnp.float32)
    if shards:
        values = values * block_scale(stream_key, shape, shards, -0.22, 0.18)
    return jnp.clip(values, -most, most).astype(kind)


def setup_inputs(seed: int = 0) -> dict:
    seeds = jax.random.split(jax.random.key(seed), 12)
    head_outputs = bell_draw(seeds[0], (TOKENS, D), 1.0, 6.0, ((0, 256),))
    residual = bell_draw(seeds[1], (TOKENS, D), 0.5, 4.0, ((0, 256),))
    output_weight = bell_draw(seeds[2], (D, D), D ** -0.5, 0.1875, ((0, 8),))
    router = bell_draw(seeds[3], (D, EXPERTS), 0.016, 0.095703125)
    norm_gain = jnp.clip(1.0 + 0.18 * jax.random.normal(seeds[4], (D,), jnp.float32), 0.1, 1.9)
    placed_gate_up = bell_draw(seeds[5], (PL, D, 2 * FF), D ** -0.5, 0.1875, ((0, 32), (1, 8)))
    placed_down = bell_draw(seeds[6], (PL, FF, D), FF ** -0.5, 0.25, ((0, 32), (1, 8)))
    routes_keys = jax.random.split(jax.random.fold_in(seeds[7], 1), TOKENS // TOK_DEV)
    routes_turns = jax.random.permutation(jax.random.fold_in(seeds[7], 3), TOKENS // TOK_DEV)
    routes = jax.vmap(lambda own, number: deal_out(jax.random.fold_in(seeds[7], 2), own, number, TOK_DEV, EXPERTS, TOP, CAP, 2))(routes_keys, routes_turns).reshape((TOKENS, TOP))
    replica_pick = plant(jax.random.randint(seeds[8], (TOKENS, TOP), 0, 6), jax.random.fold_in(seeds[8], 1), 0, 5).astype(jnp.int32)
    placement = draw_placement(jax.random.fold_in(seeds[11], 71), 0)
    final_gain = jnp.clip(1.0 + 0.18 * jax.random.normal(seeds[10], (D,), jnp.float32), 0.1, 1.9)
    return {"head_outputs": head_outputs, "residual": residual, "output_weight": output_weight, "router": router, "norm_gain": norm_gain, "placed_gate_up": placed_gate_up, "placed_down": placed_down, "routes": routes, "replica_pick": replica_pick, "placement": placement, "final_gain": final_gain}


eps_norm = 1e-06
most_copies = 3

def rms_scale(values, scale_gain):
    mean_square = lax.optimization_barrier(jnp.mean(values * values, axis=-1, keepdims=True))
    return values * lax.rsqrt(mean_square + eps_norm) * scale_gain

def choose_slots(routes, replica_pick, placement, experts):
    labels = jnp.arange(experts, dtype=jnp.int32)
    holder_mask = (placement[None, :] == labels[:, None]).astype(jnp.int32)
    before = (jnp.cumsum(holder_mask, axis=1) - holder_mask).astype(jnp.int32)
    copies = lax.optimization_barrier(jnp.sum(holder_mask, axis=1)).astype(jnp.int32)
    places = jnp.arange(placement.shape[0], dtype=jnp.int32)
    route_hits = (routes[..., None] == labels).astype(jnp.int32)
    held_count = lax.optimization_barrier(jnp.sum(route_hits * copies, axis=-1)).astype(jnp.int32)
    wanted = (replica_pick % held_count).astype(jnp.int32)
    chosen = jnp.zeros(routes.shape, jnp.int32)
    for replica in range(most_copies):
        column = lax.optimization_barrier(jnp.sum(holder_mask * (before == replica).astype(jnp.int32) * places[None, :], axis=1)).astype(jnp.int32)
        candidate = lax.optimization_barrier(jnp.sum(route_hits * column, axis=-1)).astype(jnp.int32)
        chosen = jnp.where(wanted == replica, candidate, chosen)
    return chosen

def expert_block(block_rows, gate_up_weight, down_weight):
    both_parts = jnp.dot(block_rows.astype(jnp.float32), gate_up_weight.astype(jnp.float32))
    hidden_units = down_weight.shape[0]
    activated = (jax.nn.silu(both_parts[:, :hidden_units]) * both_parts[:, hidden_units:]).astype(jnp.bfloat16)
    return jnp.dot(activated.astype(jnp.float32), down_weight.astype(jnp.float32)).astype(jnp.bfloat16)

def reference(head_outputs, residual, output_weight, router, norm_gain, placed_gate_up, placed_down, routes, replica_pick, placement, final_gain):
    projected = jnp.dot(head_outputs.astype(jnp.float32), output_weight.astype(jnp.float32))
    hidden = (residual.astype(jnp.float32) + projected).astype(jnp.bfloat16)
    hidden_wide = hidden.astype(jnp.float32)
    normed = rms_scale(hidden_wide, norm_gain).astype(jnp.bfloat16)
    logits = jnp.dot(normed.astype(jnp.float32), router.astype(jnp.float32))
    labels = jnp.arange(EXPERTS, dtype=jnp.int32)
    selector = (routes[..., None] == labels).astype(jnp.float32)
    chosen_logits = lax.optimization_barrier(jnp.sum(selector * logits[:, None, :], axis=-1))
    raised = jnp.exp(chosen_logits)
    route_weight = raised / lax.optimization_barrier(jnp.sum(raised, axis=-1, keepdims=True))
    slot_ids = choose_slots(routes, replica_pick, placement, EXPERTS).reshape(-1)
    count_all = TOKENS * TOP
    counts = jnp.zeros((PL,), jnp.int32).at[slot_ids].add(jnp.ones((count_all,), jnp.int32))
    sort_order = jnp.argsort(slot_ids, stable=True).astype(jnp.int32)
    sorted_slots = slot_ids[sort_order]
    firsts = (jnp.cumsum(counts) - counts).astype(jnp.int32)
    rank_sorted = (jnp.arange(count_all, dtype=jnp.int32) - firsts[sorted_slots]).astype(jnp.int32)
    slot_rank = jnp.zeros((count_all,), jnp.int32).at[sort_order].set(rank_sorted)
    block_size = 512
    padded_len = ((counts + block_size - 1) // block_size * block_size).astype(jnp.int32)
    padded_start = (jnp.cumsum(padded_len) - padded_len).astype(jnp.int32)
    position = (padded_start[slot_ids] + slot_rank).astype(jnp.int32)
    block_count = count_all // block_size + PL
    owner_table = jnp.full((block_count * block_size,), -1, jnp.int32).at[position].set(jnp.arange(count_all, dtype=jnp.int32))
    owner_table = owner_table.reshape(block_count, block_size)
    slot_ends = padded_start + padded_len
    block_starts = jnp.arange(block_count, dtype=jnp.int32) * block_size
    block_slot = jnp.minimum(lax.optimization_barrier(jnp.sum((slot_ends[None, :] <= block_starts[:, None]).astype(jnp.int32), axis=1)), PL - 1).astype(jnp.int32)
    flat_weight = route_weight.reshape(-1)

    def add_block(running_sum, item_pair):
        owner_ids, slot_here = item_pair
        is_live = owner_ids >= 0
        safe_ids = jnp.maximum(owner_ids, 0).astype(jnp.int32)
        row_ids = (safe_ids // TOP).astype(jnp.int32)
        block_out = expert_block(normed[row_ids], placed_gate_up[slot_here], placed_down[slot_here])
        weighted = jnp.where(is_live[:, None], flat_weight[safe_ids][:, None] * block_out.astype(jnp.float32), jnp.zeros((), jnp.float32))
        return (running_sum.at[row_ids].add(weighted), None)
    mixture, _ = lax.scan(add_block, jnp.zeros((TOKENS, D), jnp.float32), (owner_table, block_slot))
    return rms_scale(hidden_wide + mixture, final_gain).astype(jnp.bfloat16)
```

```python
import functools

import jax
import jax.numpy as jnp
from jax import lax
from jax.experimental import pallas as pl
from jax.experimental.pallas import tpu as pltpu
from jax.sharding import PartitionSpec as P

NX, NY, NZ = 4, 4, 8
CHIPS = NX * NY
D = 1024
FF = 512
EXPERTS = 32
TOP = 8
TOK = 128
CAP = 48
PL = 64
QW = 256
HALF = FF // 2
SLOTS = 4
ROWS = CHIPS * CAP
EPS = 1e-06
MESH = pl.DeviceIdType.MESH
BF = jnp.bfloat16
F32 = jnp.float32
ZHOPS = ((4, 3), (3, 4))
PHOPS = ((2, 1), (1, 2))
NT = (((1,), (1,)), ((), ()))
TN = (((0,), (0,)), ((), ()))


def wrap(v, n):
    return lax.rem(v + n, n)


def rms(values, gain):
    mean_square = jnp.mean(values * values, axis=-1, keepdims=True)
    return values * lax.rsqrt(mean_square + EPS) * gain


def body_kernel(
    ho,
    res,
    wo_in,
    gu_in,
    dn_in,
    router,
    ngain,
    fgain,
    routes,
    pick,
    plc,
    out_ref,
    ho_v,
    res_v,
    wo,
    wgu,
    wd,
    xq,
    xc,
    act,
    yc,
    part,
    rb1,
    rb2,
    hid,
    wt,
    pw,
    lsem,
    o_r,
    o_s,
    op_r,
    op_s,
    z_r,
    z_s,
    zp_r,
    zp_s,
    a1_r,
    a1_s,
    a2_r,
    a2_s,
    r1_r,
    r1_s,
    r2_r,
    r2_s,
):
    e = lax.axis_index("expert")
    z = lax.axis_index("shard")
    chip = lax.div(e, 2)
    core = lax.rem(e, 2)
    x = lax.div(chip, NY)
    y = lax.rem(chip, NY)

    def dev(xx, yy, zz, cc):
        return ((xx * NY + yy) * 2 + cc, zz)

    partner = dev(x, y, z, 1 - core)
    znb = (dev(x, y, wrap(z + 1, NZ), core), dev(x, y, wrap(z - 1, NZ), core))
    xnb = (dev(wrap(x + 1, NX), y, z, core), dev(wrap(x - 1, NX), y, z, core))
    ynb = (dev(x, wrap(y + 1, NY), z, core), dev(x, wrap(y - 1, NY), z, core))

    sends = []

    def send(src, dst, ssem, rsem, to):
        copy = pltpu.make_async_remote_copy(
            src_ref=src, dst_ref=dst, send_sem=ssem, recv_sem=rsem, device_id=to, device_id_type=MESH
        )
        copy.start()
        sends.append(copy)

    def arrived(dst, ssem, rsem):
        pltpu.make_async_remote_copy(
            src_ref=dst, dst_ref=dst, send_sem=ssem, recv_sem=rsem, device_id=partner, device_id_type=MESH
        ).wait_recv()

    zrow = pl.ds(pl.multiple_of(z * 128, 128), 128)
    zrow2 = pl.ds(pl.multiple_of(z * 64, 64), 64)
    local = []

    def load(src, dst):
        copy = pltpu.make_async_copy(src, dst, lsem.at[len(local)])
        copy.start()
        local.append(copy)

    for q in range(4):
        load(wo_in.at[:, pl.ds(q * QW, QW)], wo.at[q, zrow, :])
    load(ho, ho_v)
    load(res, res_v)
    for c in range(2):
        for j in range(2):
            s = 2 * core + j
            load(gu_in.at[j, :, pl.ds(c * HALF, HALF)], wgu.at[c, s, zrow, pl.ds(0, HALF)])
            load(gu_in.at[j, :, pl.ds(FF + c * HALF, HALF)], wgu.at[c, s, zrow, pl.ds(HALF, HALF)])
    for j in range(2):
        load(dn_in.at[j], wd.at[2 * core + j, zrow2, :])

    barrier = pltpu.get_barrier_semaphore()
    for nb in (partner,) + znb + xnb + ynb:
        pl.semaphore_signal(barrier, inc=1, device_id=nb, device_id_type=MESH)
    pl.semaphore_wait(barrier, 7)

    for copy in local:
        copy.wait()

    def shard_of(dirn, k):
        return wrap(z - k, NZ) if dirn == 0 else wrap(z + k, NZ)

    class Ring:
        def __init__(self, where, hops, s_sem, r_sem, ps_sem, pr_sem, share_own):
            self.where, self.hops = where, hops
            self.s_sem, self.r_sem, self.ps_sem, self.pr_sem = s_sem, r_sem, ps_sem, pr_sem
            self.share_own = share_own

        def go(self, dirn, k):
            at = self.where(core, shard_of(dirn, k))
            i = dirn * 4 + k
            send(at, at, self.s_sem(i), self.r_sem(i), znb[dirn])

        def begin(self):
            self.go(0, 0)
            self.go(1, 0)
            if self.share_own:
                at = self.where(core, z)
                send(at, at, self.ps_sem(8), self.pr_sem(8), partner)

        def arrive(self, k):
            for dirn in range(2):
                if k < self.hops[dirn]:
                    i = dirn * 4 + k
                    at = self.where(core, shard_of(dirn, k + 1))
                    arrived(at, self.s_sem(i), self.r_sem(i))
                    if k + 1 < self.hops[dirn]:
                        self.go(dirn, k + 1)
                    send(at, at, self.ps_sem(i), self.pr_sem(i), partner)

        def from_partner(self):
            other = 1 - core
            for dirn in range(2):
                for k in range(self.hops[dirn]):
                    i = dirn * 4 + k
                    arrived(self.where(other, shard_of(dirn, k + 1)), self.ps_sem(i), self.pr_sem(i))
            if self.share_own:
                arrived(self.where(other, z), self.ps_sem(8), self.pr_sem(8))

    def wo_at(i):
        return lambda cc, zz: wo.at[2 * cc + i, pl.ds(pl.multiple_of(zz * 128, 128), 128), :]

    def gu_at(c, j):
        return lambda cc, zz: wgu.at[c, 2 * cc + j, pl.ds(pl.multiple_of(zz * 128, 128), 128), :]

    def dn_at(j):
        return lambda cc, zz: wd.at[2 * cc + j, pl.ds(pl.multiple_of(zz * 64, 64), 64), :]

    def sem_row(ref, u):
        return lambda i: ref.at[u, i]

    def ring(where, u, hops, refs, own):
        return Ring(where, hops, *[sem_row(r, u) for r in refs], own)

    orings = [ring(wo_at(i), i, ZHOPS[i], (o_s, o_r, op_s, op_r), False) for i in range(2)]
    zrefs = (z_s, z_r, zp_s, zp_r)
    pieces = [
        [ring(gu_at(0, j), j, ZHOPS[j], zrefs, True) for j in range(2)],
        [ring(dn_at(j), 2 + j, ZHOPS[j], zrefs, True) for j in range(2)],
        [ring(gu_at(1, j), 4 + j, ZHOPS[j], zrefs, True) for j in range(2)],
    ]

    def z_begin(p):
        for r in pieces[p]:
            r.begin()

    def z_arrive(p, k):
        for r in pieces[p]:
            r.arrive(k)

    zqueue = [
        lambda: z_arrive(0, 0),
        lambda: z_arrive(1, 0),
        lambda: (z_arrive(0, 1), z_begin(2)),
        lambda: z_arrive(1, 1),
        lambda: z_arrive(0, 2),
        lambda: z_arrive(2, 0),
        lambda: z_arrive(1, 2),
        lambda: z_arrive(0, 3),
        lambda: z_arrive(2, 1),
        lambda: z_arrive(1, 3),
        lambda: z_arrive(2, 2),
        lambda: z_arrive(2, 3),
    ]

    def pump():
        if zqueue:
            zqueue.pop(0)()

    for r in orings:
        r.begin()
    for k in range(3):
        for r in orings:
            r.arrive(k)
    z_begin(0)
    z_begin(1)

    plc_row = plc[...].astype(F32)
    rows64 = lax.broadcasted_iota(jnp.int32, (PL, PL), 0)
    cols64 = lax.broadcasted_iota(jnp.int32, (PL, PL), 1)
    plc_col = jnp.sum(jnp.where(rows64 == cols64, plc_row, 0.0), axis=1, keepdims=True)
    same = plc_col == plc_row
    copies = jnp.sum(jnp.where(same, 1.0, 0.0), axis=1, keepdims=True)
    order = jnp.sum(jnp.where(same & (cols64 < rows64), 1.0, 0.0), axis=1, keepdims=True)
    eye8 = (
        lax.broadcasted_iota(jnp.int32, (TOP, TOP), 0) == lax.broadcasted_iota(jnp.int32, (TOP, TOP), 1)
    ).astype(BF)
    routes_t = lax.dot_general(eye8, routes[...].astype(BF), NT, preferred_element_type=F32)
    pick_t = lax.dot_general(eye8, pick[...].astype(BF), NT, preferred_element_type=F32)
    hit = jnp.zeros((PL, TOK), F32)
    for k in range(TOP):
        route = routes_t[k : k + 1, :]
        p = pick_t[k : k + 1, :]
        by2 = p - jnp.where(p >= 2.0, 2.0, 0.0) - jnp.where(p >= 4.0, 2.0, 0.0)
        by3 = p - jnp.where(p >= 3.0, 3.0, 0.0)
        wanted = jnp.where(copies == 1.0, 0.0, jnp.where(copies == 2.0, by2, by3))
        hit = hit + jnp.where((route == plc_col) & (wanted == order), 1.0, 0.0)
    names = (plc_col == lax.broadcasted_iota(jnp.int32, (PL, EXPERTS), 1).astype(F32)).astype(BF)
    router_rows = lax.dot_general(names, router[...], NT, preferred_element_type=F32).astype(BF)

    for r in orings:
        r.arrive(3)
    for r in orings:
        r.from_partner()

    for q in range(4):
        cols = pl.ds(q * QW, QW)
        projected = jnp.dot(ho_v[...], wo[q], preferred_element_type=F32)
        hid[:, cols] = (res_v[:, cols].astype(F32) + projected).astype(BF)
    normed = rms(hid[...].astype(F32), ngain[...]).astype(BF)
    logits = lax.dot_general(router_rows, normed, NT, preferred_element_type=F32)
    raised = jnp.where(hit > 0.0, jnp.exp(logits), 0.0)
    weight = (raised / jnp.sum(raised, axis=0, keepdims=True)).astype(BF)
    for q in range(4):
        xq[q, chip, 0:TOK, :] = normed[:, q * QW : (q + 1) * QW]
    xq[0, chip, TOK : TOK + 32, 0:128] = weight[0:32, :]
    xq[0, chip, TOK : TOK + 32, 128:256] = weight[32:64, :]

    def axes(q):
        return (x, y, xnb, ynb) if q < 2 else (y, x, ynb, xnb)

    def cid(q, aa, bb):
        return aa * NY + bb if q < 2 else bb * NY + aa

    def block(q, idx):
        return xq.at[q, idx, pl.ds(0, TOK + 32 if q == 0 else TOK), :]

    def back(v, dirn, k):
        return wrap(v - k, 4) if dirn == 0 else wrap(v + k, 4)

    def hop_index(q, dirn, k):
        return k if dirn == 0 else PHOPS[q % 2][0] + k

    def a1_go(q, dirn, k):
        a, b, na, nb = axes(q)
        at = block(q, cid(q, back(a, dirn, k), b))
        i = hop_index(q, dirn, k)
        send(at, at, a1_s.at[q, i], a1_r.at[q, i], na[dirn])

    def a2_go(q, label, aa, dirn, k):
        a, b, na, nb = axes(q)
        at = block(q, cid(q, aa, back(b, dirn, k)))
        i = hop_index(q, dirn, k)
        send(at, at, a2_s.at[q, label, i], a2_r.at[q, label, i], nb[dirn])

    def a1_arrive(q, dirn, k):
        a, b, na, nb = axes(q)
        aa = back(a, dirn, k + 1)
        i = hop_index(q, dirn, k)
        arrived(block(q, cid(q, aa, b)), a1_s.at[q, i], a1_r.at[q, i])
        if k + 1 < PHOPS[q % 2][dirn]:
            a1_go(q, dirn, k + 1)
        for d2 in range(2):
            a2_go(q, 1 + i, aa, d2, 0)

    def a2_arrive(q, label, aa, dirn, k):
        a, b, na, nb = axes(q)
        i = hop_index(q, dirn, k)
        arrived(block(q, cid(q, aa, back(b, dirn, k + 1))), a2_s.at[q, label, i], a2_r.at[q, label, i])
        if k + 1 < PHOPS[q % 2][dirn]:
            a2_go(q, label, aa, dirn, k + 1)

    for q in range(4):
        a = axes(q)[0]
        for dirn in range(2):
            a1_go(q, dirn, 0)
        for dirn in range(2):
            a2_go(q, 0, a, dirn, 0)
    events = []
    for q in range(4):
        a = axes(q)[0]
        hops = [(dirn, k) for dirn in range(2) for k in range(PHOPS[q % 2][dirn])]
        for d2, k2 in hops:
            events.append((k2 + 1, q, functools.partial(a2_arrive, q, 0, a, d2, k2)))
        for dirn, k in hops:
            events.append((k + 1, q, functools.partial(a1_arrive, q, dirn, k)))
            aa = back(a, dirn, k + 1)
            label = 1 + hop_index(q, dirn, k)
            for d2, k2 in hops:
                events.append((k + k2 + 2, q, functools.partial(a2_arrive, q, label, aa, d2, k2)))
    events.sort(key=lambda ev: ev[:2])
    for n, (_, _, run) in enumerate(events):
        run()
        if n % 15 == 14:
            pump()

    lane32 = lax.broadcasted_iota(jnp.int32, (TOP, 32), 1)
    row32 = lax.broadcasted_iota(jnp.int32, (TOP, 32), 0)
    mine = SLOTS * chip + row32
    pick_lo = ((lane32 == mine) & (row32 < SLOTS)).astype(BF)
    pick_hi = ((lane32 + 32 == mine) & (row32 < SLOTS)).astype(BF)

    def take_weights(s, carry):
        table = xq[0, s, TOK : TOK + 32, :]
        wt[pl.ds(pl.multiple_of(s * 8, 8), 8), :] = jnp.dot(
            pick_lo, table[:, 0:128], preferred_element_type=F32
        ) + jnp.dot(pick_hi, table[:, 128:256], preferred_element_type=F32)
        return carry

    lax.fori_loop(0, CHIPS, take_weights, 0)
    weights = wt[0:128, :]
    rows128 = lax.broadcasted_iota(jnp.int32, (TOK, TOK), 0)
    cols128 = lax.broadcasted_iota(jnp.int32, (TOK, TOK), 1)
    earlier = (rows128 < cols128).astype(BF)
    taken = weights > 0.0
    rank = jnp.dot(taken.astype(BF), earlier, preferred_element_type=F32)
    wt[pl.ds(128, 128), :] = jnp.where(taken, rank, -1.0)

    def compact(s, carry):
        base = pl.multiple_of(s * 8, 8)
        w8 = wt[pl.ds(base, 8), :]
        r8 = wt[pl.ds(pl.multiple_of(128 + s * 8, 8), 8), :]
        rows = lax.broadcasted_iota(jnp.int32, (CAP, TOK), 0).astype(F32)
        here = [rows == r8[j : j + 1, :] for j in range(SLOTS)]
        chosen = jnp.concatenate([jnp.where(h, 1.0, 0.0) for h in here], axis=0).astype(BF)
        pw[s] = jnp.concatenate(
            [jnp.where(here[j], w8[j : j + 1, :], 0.0) for j in range(SLOTS)], axis=0
        ).astype(BF)
        tokens = jnp.concatenate([xq[q, s, 0:TOK, :] for q in range(4)], axis=1)
        packed = jnp.dot(chosen, tokens, preferred_element_type=F32).astype(BF)
        for j in range(SLOTS):
            xc[j, pl.ds(pl.multiple_of(s * CAP, 16), CAP), :] = packed[j * CAP : (j + 1) * CAP, :]
        return carry

    for g in range(2):
        lax.fori_loop(g * 8, g * 8 + 8, compact, 0)
        pump()

    def gate_up(c, n, carry):
        j = lax.div(n, 3)
        at = pl.ds(pl.multiple_of(lax.rem(n, 3) * 256, 256), 256)
        both = jnp.dot(xc[j, at, :], wgu[c, j], preferred_element_type=F32)
        g, u = both[:, 0:HALF], both[:, HALF:]
        act[j, at, c * HALF : (c + 1) * HALF] = (g / (1.0 + jnp.exp(-g)) * u).astype(BF)
        return carry

    while len(zqueue) > 4:
        pump()
    for r in pieces[0]:
        r.from_partner()
    for g in range(2):
        lax.fori_loop(g * 6, g * 6 + 6, functools.partial(gate_up, 0), 0)
        pump()
    while zqueue:
        pump()
    for r in pieces[1] + pieces[2]:
        r.from_partner()
    lax.fori_loop(0, 12, functools.partial(gate_up, 1), 0)

    def down(n, carry):
        j = lax.div(n, 3)
        at = pl.ds(pl.multiple_of(lax.rem(n, 3) * 256, 256), 256)
        yc[j, at, :] = jnp.dot(act[j, at, :], wd[j], preferred_element_type=F32).astype(BF)
        return carry

    lax.fori_loop(0, 12, down, 0)

    def combine(s, carry):
        at = pl.ds(pl.multiple_of(s * CAP, 16), CAP)
        outs = jnp.concatenate([yc[j, at, :] for j in range(SLOTS)], axis=0)
        total = lax.dot_general(pw[s], outs, TN, preferred_element_type=F32).astype(BF)
        for q in range(4):
            part[q, s] = total[:, q * QW : (q + 1) * QW]
        return carry

    lax.fori_loop(0, CHIPS, combine, 0)

    def ahead(v, h, dirn, k):
        left = h - k
        return wrap(v + left, 4) if dirn == 0 else wrap(v - left, 4)

    def s1_go(q, o, dirn, k):
        a, b, na, nb = axes(q)
        i = hop_index(q, dirn, k)
        target = cid(q, ahead(a, PHOPS[q % 2][dirn], dirn, k), wrap(b + o, 4))
        send(part.at[q, target], rb1.at[q, i, o], r1_s.at[q, i, o], r1_r.at[q, i, o], na[dirn])

    def s2_go(q, dirn, k):
        a, b, na, nb = axes(q)
        i = hop_index(q, dirn, k)
        target = cid(q, a, ahead(b, PHOPS[q % 2][dirn], dirn, k))
        send(part.at[q, target], rb2.at[q, i], r2_s.at[q, i], r2_r.at[q, i], nb[dirn])

    def s1_wait(q, o, dirn, k):
        i = hop_index(q, dirn, k)
        arrived(rb1.at[q, i, o], r1_s.at[q, i, o], r1_r.at[q, i, o])
        return rb1[q, i, o].astype(F32)

    def s2_wait(q, dirn, k):
        i = hop_index(q, dirn, k)
        arrived(rb2.at[q, i], r2_s.at[q, i], r2_r.at[q, i])
        return rb2[q, i].astype(F32)

    def add_into(q, idx, *terms):
        total = part[q, idx].astype(F32)
        for t in terms:
            total = total + t
        part[q, idx] = total.astype(BF)

    offsets = (2, 1, 3, 0)
    for o in offsets:
        for q in range(4):
            for dirn in range(2):
                s1_go(q, o, dirn, 0)
    for o in offsets:
        for q in range(4):
            a, b, na, nb = axes(q)
            far = 0 if PHOPS[q % 2][0] == 2 else 1
            add_into(q, cid(q, ahead(a, 2, far, 1), wrap(b + o, 4)), s1_wait(q, o, far, 0))
            s1_go(q, o, far, 1)
    own = [None] * 4
    for o in offsets:
        for q in range(4):
            a, b, na, nb = axes(q)
            right, left = PHOPS[q % 2]
            terms = [s1_wait(q, o, 0, right - 1), s1_wait(q, o, 1, left - 1)]
            far = 0 if right == 2 else 1
            mid = 1 if far == 0 else 3
            add_into(q, cid(q, a, wrap(b + o, 4)), *terms)
            if o == 2:
                s2_go(q, far, 0)
            elif o == 4 - mid:
                s2_go(q, 1 - far, 0)
    for q in range(4):
        a, b, na, nb = axes(q)
        far = 0 if PHOPS[q % 2][0] == 2 else 1
        add_into(q, cid(q, a, ahead(b, 2, far, 1)), s2_wait(q, far, 0))
        s2_go(q, far, 1)
    for q in range(4):
        right, left = PHOPS[q % 2]
        own[q] = part[q, chip].astype(F32) + s2_wait(q, 0, right - 1) + s2_wait(q, 1, left - 1)
    mixture = jnp.concatenate(own, axis=1)
    out_ref[...] = rms(hid[...].astype(F32) + mixture, fgain[...]).astype(BF)

    for copy in sends:
        copy.wait_send()


def body(
    head_outputs,
    residual,
    output_weight,
    router,
    norm_gain,
    placed_gate_up,
    placed_down,
    routes,
    replica_pick,
    placement,
    final_gain,
):
    dma = pltpu.SemaphoreType.DMA
    anywhere = pl.BlockSpec(memory_space=pl.ANY)
    vmem = pl.BlockSpec(memory_space=pltpu.VMEM)
    return pl.pallas_call(
        body_kernel,
        out_shape=jax.ShapeDtypeStruct((TOK, D), BF),
        in_specs=[anywhere] * 5 + [vmem] * 6,
        out_specs=vmem,
        scratch_shapes=[
            pltpu.VMEM((TOK, D), BF),
            pltpu.VMEM((TOK, D), BF),
            pltpu.VMEM((4, D, QW), BF),
            pltpu.VMEM((2, SLOTS, D, FF), BF),
            pltpu.VMEM((SLOTS, FF, D), BF),
            pltpu.VMEM((4, CHIPS, TOK + 32, QW), BF),
            pltpu.VMEM((SLOTS, ROWS, D), BF),
            pltpu.VMEM((SLOTS, ROWS, FF), BF),
            pltpu.VMEM((SLOTS, ROWS, D), BF),
            pltpu.VMEM((4, CHIPS, TOK, QW), BF),
            pltpu.VMEM((4, 3, 4, TOK, QW), BF),
            pltpu.VMEM((4, 3, TOK, QW), BF),
            pltpu.VMEM((TOK, D), BF),
            pltpu.VMEM((256, TOK), F32),
            pltpu.VMEM((CHIPS, SLOTS * CAP, TOK), BF),
            dma((16,)),
            dma((2, 8)),
            dma((2, 8)),
            dma((2, 8)),
            dma((2, 8)),
            dma((6, 8)),
            dma((6, 8)),
            dma((6, 9)),
            dma((6, 9)),
            dma((4, 3)),
            dma((4, 3)),
            dma((4, 4, 3)),
            dma((4, 4, 3)),
            dma((4, 3, 4)),
            dma((4, 3, 4)),
            dma((4, 3)),
            dma((4, 3)),
        ],
        compiler_params=pltpu.CompilerParams(
            collective_id=0, has_side_effects=True, vmem_limit_bytes=60 * 1024 * 1024
        ),
    )(
        head_outputs,
        residual,
        output_weight,
        placed_gate_up,
        placed_down,
        router,
        norm_gain.reshape(1, D),
        final_gain.reshape(1, D),
        routes,
        replica_pick,
        placement.reshape(1, PL),
    )


def solution(mesh):
    return jax.shard_map(
        body,
        mesh=mesh,
        in_specs=(
            P(("expert", "shard"), None),
            P(("expert", "shard"), None),
            P("shard", None),
            P(),
            P(),
            P("expert", "shard", None),
            P("expert", "shard", None),
            P(("expert", "shard"), None),
            P(("expert", "shard"), None),
            P(),
            P(),
        ),
        out_specs=P(("expert", "shard"), None),
        check_vma=False,
    )
```

```python
import functools

import jax
import jax.numpy as jnp
from jax import lax
from jax.experimental import pallas as pl
from jax.experimental.pallas import tpu as pltpu
from jax.sharding import PartitionSpec as P

NX, NY, NZ = 4, 4, 8
CHIPS = NX * NY
D = 1024
FF = 512
EXPERTS = 32
TOP = 8
TOK = 128
CAP = 48
PL = 64
QW = 256
HW = 512
HALF = FF // 2
SLOTS = 4
ROWS = CHIPS * CAP
EPS = 1e-06
MESH = pl.DeviceIdType.MESH
BF = jnp.bfloat16
F32 = jnp.float32
ZHOPS = ((4, 3), (3, 4))
PHOPS = ((2, 1), (1, 2), (1, 2), (2, 1))
NT = (((1,), (1,)), ((), ()))
TN = (((0,), (0,)), ((), ()))


def wrap(v, n):
    return lax.rem(v + n, n)


def rms(values, gain):
    mean_square = jnp.mean(values * values, axis=-1, keepdims=True)
    return values * lax.rsqrt(mean_square + EPS) * gain


def body_kernel(
    ho,
    res,
    wo_in,
    gu_in,
    dn_in,
    router,
    ngain,
    fgain,
    routes,
    pick,
    plc,
    out_ref,
    ho_v,
    res_v,
    wo,
    wgu,
    wd,
    xq,
    xc,
    act,
    yc,
    part,
    rb1,
    rb2,
    hid,
    wt,
    pw,
    lsem,
    o_r,
    o_s,
    op_r,
    op_s,
    z_r,
    z_s,
    zp_r,
    zp_s,
    a1_r,
    a1_s,
    a2_r,
    a2_s,
    r1_r,
    r1_s,
    r2_r,
    r2_s,
):
    e = lax.axis_index("expert")
    z = lax.axis_index("shard")
    chip = lax.div(e, 2)
    core = lax.rem(e, 2)
    x = lax.div(chip, NY)
    y = lax.rem(chip, NY)

    def dev(xx, yy, zz, cc):
        return ((xx * NY + yy) * 2 + cc, zz)

    partner = dev(x, y, z, 1 - core)
    znb = (dev(x, y, wrap(z + 1, NZ), core), dev(x, y, wrap(z - 1, NZ), core))
    xnb = (dev(wrap(x + 1, NX), y, z, core), dev(wrap(x - 1, NX), y, z, core))
    ynb = (dev(x, wrap(y + 1, NY), z, core), dev(x, wrap(y - 1, NY), z, core))

    sends = []

    def send(src, dst, ssem, rsem, to):
        copy = pltpu.make_async_remote_copy(
            src_ref=src, dst_ref=dst, send_sem=ssem, recv_sem=rsem, device_id=to, device_id_type=MESH
        )
        copy.start()
        sends.append(copy)

    def arrived(dst, ssem, rsem):
        pltpu.make_async_remote_copy(
            src_ref=dst, dst_ref=dst, send_sem=ssem, recv_sem=rsem, device_id=partner, device_id_type=MESH
        ).wait_recv()

    zrow = pl.ds(pl.multiple_of(z * 128, 128), 128)
    zrow2 = pl.ds(pl.multiple_of(z * 64, 64), 64)
    local = []

    def load(src, dst):
        copy = pltpu.make_async_copy(src, dst, lsem.at[len(local)])
        copy.start()
        local.append(copy)

    for q in range(4):
        load(wo_in.at[:, pl.ds(q * QW, QW)], wo.at[q, zrow, :])
    load(ho, ho_v)
    load(res, res_v)
    for c in range(2):
        for j in range(2):
            s = 2 * core + j
            load(gu_in.at[j, :, pl.ds(c * HALF, HALF)], wgu.at[c, s, zrow, pl.ds(0, HALF)])
            load(gu_in.at[j, :, pl.ds(FF + c * HALF, HALF)], wgu.at[c, s, zrow, pl.ds(HALF, HALF)])
    for h in range(2):
        for j in range(2):
            load(dn_in.at[j, :, pl.ds(h * HW, HW)], wd.at[h, 2 * core + j, zrow2, :])

    barrier = pltpu.get_barrier_semaphore()
    for nb in (partner,) + znb + xnb + ynb:
        pl.semaphore_signal(barrier, inc=1, device_id=nb, device_id_type=MESH)
    pl.semaphore_wait(barrier, 7)

    for copy in local:
        copy.wait()

    def shard_of(dirn, k):
        return wrap(z - k, NZ) if dirn == 0 else wrap(z + k, NZ)

    class Ring:
        def __init__(self, where, hops, s_sem, r_sem, ps_sem, pr_sem, share_own):
            self.where, self.hops = where, hops
            self.s_sem, self.r_sem, self.ps_sem, self.pr_sem = s_sem, r_sem, ps_sem, pr_sem
            self.share_own = share_own

        def go(self, dirn, k):
            at = self.where(core, shard_of(dirn, k))
            i = dirn * 4 + k
            send(at, at, self.s_sem(i), self.r_sem(i), znb[dirn])

        def begin(self):
            self.go(0, 0)
            self.go(1, 0)
            if self.share_own:
                at = self.where(core, z)
                send(at, at, self.ps_sem(8), self.pr_sem(8), partner)

        def arrive(self, k):
            for dirn in range(2):
                if k < self.hops[dirn]:
                    i = dirn * 4 + k
                    at = self.where(core, shard_of(dirn, k + 1))
                    arrived(at, self.s_sem(i), self.r_sem(i))
                    if k + 1 < self.hops[dirn]:
                        self.go(dirn, k + 1)
                    send(at, at, self.ps_sem(i), self.pr_sem(i), partner)

        def from_partner(self):
            other = 1 - core
            for dirn in range(2):
                for k in range(self.hops[dirn]):
                    i = dirn * 4 + k
                    arrived(self.where(other, shard_of(dirn, k + 1)), self.ps_sem(i), self.pr_sem(i))
            if self.share_own:
                arrived(self.where(other, z), self.ps_sem(8), self.pr_sem(8))

    def wo_at(i):
        return lambda cc, zz: wo.at[2 * cc + i, pl.ds(pl.multiple_of(zz * 128, 128), 128), :]

    def gu_at(c, j):
        return lambda cc, zz: wgu.at[c, 2 * cc + j, pl.ds(pl.multiple_of(zz * 128, 128), 128), :]

    def dn_at(h, j):
        return lambda cc, zz: wd.at[h, 2 * cc + j, pl.ds(pl.multiple_of(zz * 64, 64), 64), :]

    def sem_row(ref, u):
        return lambda i: ref.at[u, i]

    def ring(where, u, hops, refs, own):
        return Ring(where, hops, *[sem_row(r, u) for r in refs], own)

    orings = [ring(wo_at(i), i, ZHOPS[i], (o_s, o_r, op_s, op_r), False) for i in range(2)]
    zrefs = (z_s, z_r, zp_s, zp_r)
    gu = [[ring(gu_at(c, j), 2 * c + j, ZHOPS[j], zrefs, True) for j in range(2)] for c in range(2)]
    dn = [[ring(dn_at(h, j), 4 + 2 * h + j, ZHOPS[j], zrefs, True) for j in range(2)] for h in range(2)]

    zqueue = [
        (21, gu[0], 0),
        (27, gu[1], 0),
        (32, gu[0], 1),
        (38, gu[1], 1),
        (44, gu[0], 2),
        (45, dn[0], 0),
        (49, gu[1], 2),
        (52, dn[0], 1),
        (53, dn[1], 0),
        (54, gu[0], 3),
        (57, dn[0], 2),
        (58, gu[1], 3),
        (60, dn[1], 1),
        (62, dn[0], 3),
        (64, dn[1], 2),
        (68, dn[1], 3),
    ]

    def pump(now):
        while zqueue and zqueue[0][0] <= now:
            _, rings, k = zqueue.pop(0)
            for r in rings:
                r.arrive(k)

    for r in orings:
        r.begin()
    dn[0][0].begin()
    for k in range(3):
        for r in orings:
            r.arrive(k)
        (dn[0][1], dn[1][0], dn[1][1])[k].begin()
    for r in gu[0] + gu[1]:
        r.begin()

    plc_row = plc[...].astype(F32)
    rows64 = lax.broadcasted_iota(jnp.int32, (PL, PL), 0)
    cols64 = lax.broadcasted_iota(jnp.int32, (PL, PL), 1)
    plc_col = jnp.sum(jnp.where(rows64 == cols64, plc_row, 0.0), axis=1, keepdims=True)
    same = plc_col == plc_row
    copies = jnp.sum(jnp.where(same, 1.0, 0.0), axis=1, keepdims=True)
    order = jnp.sum(jnp.where(same & (cols64 < rows64), 1.0, 0.0), axis=1, keepdims=True)
    eye8 = (
        lax.broadcasted_iota(jnp.int32, (TOP, TOP), 0) == lax.broadcasted_iota(jnp.int32, (TOP, TOP), 1)
    ).astype(BF)
    routes_t = lax.dot_general(eye8, routes[...].astype(BF), NT, preferred_element_type=F32)
    pick_t = lax.dot_general(eye8, pick[...].astype(BF), NT, preferred_element_type=F32)
    hit = jnp.zeros((PL, TOK), F32)
    for k in range(TOP):
        route = routes_t[k : k + 1, :]
        p = pick_t[k : k + 1, :]
        by2 = p - jnp.where(p >= 2.0, 2.0, 0.0) - jnp.where(p >= 4.0, 2.0, 0.0)
        by3 = p - jnp.where(p >= 3.0, 3.0, 0.0)
        wanted = jnp.where(copies == 1.0, 0.0, jnp.where(copies == 2.0, by2, by3))
        hit = hit + jnp.where((route == plc_col) & (wanted == order), 1.0, 0.0)
    names = (plc_col == lax.broadcasted_iota(jnp.int32, (PL, EXPERTS), 1).astype(F32)).astype(BF)
    router_rows = lax.dot_general(names, router[...], NT, preferred_element_type=F32).astype(BF)

    for r in orings:
        r.arrive(3)
    for r in orings:
        r.from_partner()

    for q in range(4):
        cols = pl.ds(q * QW, QW)
        projected = jnp.dot(ho_v[...], wo[q], preferred_element_type=F32)
        hid[:, cols] = (res_v[:, cols].astype(F32) + projected).astype(BF)
    normed = rms(hid[...].astype(F32), ngain[...]).astype(BF)
    logits = lax.dot_general(router_rows, normed, NT, preferred_element_type=F32)
    raised = jnp.where(hit > 0.0, jnp.exp(logits), 0.0)
    weight = (raised / jnp.sum(raised, axis=0, keepdims=True)).astype(BF)
    for q in range(4):
        xq[q, chip, 0:TOK, :] = normed[:, q * QW : (q + 1) * QW]
    xq[0, chip, TOK : TOK + 32, 0:128] = weight[0:32, :]
    xq[0, chip, TOK : TOK + 32, 128:256] = weight[32:64, :]

    def axes(q):
        return (x, y, xnb, ynb) if q % 2 == 0 else (y, x, ynb, xnb)

    def cid(q, aa, bb):
        return aa * NY + bb if q % 2 == 0 else bb * NY + aa

    def block(q, idx):
        return xq.at[q, idx, pl.ds(0, TOK + 32 if q == 0 else TOK), :]

    def back(v, dirn, k):
        return wrap(v - k, 4) if dirn == 0 else wrap(v + k, 4)

    def hop_index(q, dirn, k):
        return k if dirn == 0 else PHOPS[q][0] + k

    def a1_go(q, dirn, k):
        a, b, na, nb = axes(q)
        at = block(q, cid(q, back(a, dirn, k), b))
        i = hop_index(q, dirn, k)
        send(at, at, a1_s.at[q, i], a1_r.at[q, i], na[dirn])

    def a2_go(q, label, aa, dirn, k):
        a, b, na, nb = axes(q)
        at = block(q, cid(q, aa, back(b, dirn, k)))
        i = hop_index(q, dirn, k)
        send(at, at, a2_s.at[q, label, i], a2_r.at[q, label, i], nb[dirn])

    def a1_arrive(q, dirn, k):
        a, b, na, nb = axes(q)
        aa = back(a, dirn, k + 1)
        i = hop_index(q, dirn, k)
        arrived(block(q, cid(q, aa, b)), a1_s.at[q, i], a1_r.at[q, i])
        if k + 1 < PHOPS[q][dirn]:
            a1_go(q, dirn, k + 1)
        for d2 in range(2):
            a2_go(q, 1 + i, aa, d2, 0)

    def a2_arrive(q, label, aa, dirn, k):
        a, b, na, nb = axes(q)
        i = hop_index(q, dirn, k)
        arrived(block(q, cid(q, aa, back(b, dirn, k + 1))), a2_s.at[q, label, i], a2_r.at[q, label, i])
        if k + 1 < PHOPS[q][dirn]:
            a2_go(q, label, aa, dirn, k + 1)

    for q in range(4):
        a = axes(q)[0]
        for dirn in range(2):
            a1_go(q, dirn, 0)
        for dirn in range(2):
            a2_go(q, 0, a, dirn, 0)
    events = []
    for q in range(4):
        a = axes(q)[0]
        hops = [(dirn, k) for dirn in range(2) for k in range(PHOPS[q][dirn])]
        for d2, k2 in hops:
            events.append((k2 + 1, q, functools.partial(a2_arrive, q, 0, a, d2, k2)))
        for dirn, k in hops:
            events.append((k + 1, q, functools.partial(a1_arrive, q, dirn, k)))
            aa = back(a, dirn, k + 1)
            label = 1 + hop_index(q, dirn, k)
            for d2, k2 in hops:
                events.append((k + k2 + 2, q, functools.partial(a2_arrive, q, label, aa, d2, k2)))
    events.sort(key=lambda ev: ev[:2])
    for n, (_, _, run) in enumerate(events):
        pump(22.5 + 0.42 * n)
        run()

    lane32 = lax.broadcasted_iota(jnp.int32, (TOP, 32), 1)
    row32 = lax.broadcasted_iota(jnp.int32, (TOP, 32), 0)
    mine = SLOTS * chip + row32
    pick_lo = ((lane32 == mine) & (row32 < SLOTS)).astype(BF)
    pick_hi = ((lane32 + 32 == mine) & (row32 < SLOTS)).astype(BF)

    def take_weights(s, carry):
        table = xq[0, s, TOK : TOK + 32, :]
        wt[pl.ds(pl.multiple_of(s * 8, 8), 8), :] = jnp.dot(
            pick_lo, table[:, 0:128], preferred_element_type=F32
        ) + jnp.dot(pick_hi, table[:, 128:256], preferred_element_type=F32)
        return carry

    lax.fori_loop(0, CHIPS, take_weights, 0)
    weights = wt[0:128, :]
    rows128 = lax.broadcasted_iota(jnp.int32, (TOK, TOK), 0)
    cols128 = lax.broadcasted_iota(jnp.int32, (TOK, TOK), 1)
    earlier = (rows128 < cols128).astype(BF)
    taken = weights > 0.0
    rank = jnp.dot(taken.astype(BF), earlier, preferred_element_type=F32)
    wt[pl.ds(128, 128), :] = jnp.where(taken, rank, -1.0)

    def compact(s, carry):
        base = pl.multiple_of(s * 8, 8)
        w8 = wt[pl.ds(base, 8), :]
        r8 = wt[pl.ds(pl.multiple_of(128 + s * 8, 8), 8), :]
        rows = lax.broadcasted_iota(jnp.int32, (CAP, TOK), 0).astype(F32)
        here = [rows == r8[j : j + 1, :] for j in range(SLOTS)]
        chosen = jnp.concatenate([jnp.where(h, 1.0, 0.0) for h in here], axis=0).astype(BF)
        pw[s] = jnp.concatenate(
            [jnp.where(here[j], w8[j : j + 1, :], 0.0) for j in range(SLOTS)], axis=0
        ).astype(BF)
        tokens = jnp.concatenate([xq[q, s, 0:TOK, :] for q in range(4)], axis=1)
        packed = jnp.dot(chosen, tokens, preferred_element_type=F32).astype(BF)
        for j in range(SLOTS):
            xc[j, pl.ds(pl.multiple_of(s * CAP, 16), CAP), :] = packed[j * CAP : (j + 1) * CAP, :]
        return carry

    for g in range(4):
        lax.fori_loop(g * 4, g * 4 + 4, compact, 0)
        pump((45, 46, 50, 53)[g])

    def gate_up(c, n, carry):
        j = lax.div(n, 3)
        at = pl.ds(pl.multiple_of(lax.rem(n, 3) * 256, 256), 256)
        both = jnp.dot(xc[j, at, :], wgu[c, j], preferred_element_type=F32)
        g, u = both[:, 0:HALF], both[:, HALF:]
        act[j, at, c * HALF : (c + 1) * HALF] = (g / (1.0 + jnp.exp(-g)) * u).astype(BF)
        return carry

    pump(54)
    for r in gu[0]:
        r.from_partner()
    for g in range(2):
        lax.fori_loop(g * 6, g * 6 + 6, functools.partial(gate_up, 0), 0)
        pump((57, 60)[g])
    for r in gu[1]:
        r.from_partner()
    for g in range(2):
        lax.fori_loop(g * 6, g * 6 + 6, functools.partial(gate_up, 1), 0)
        pump((62, 64)[g])

    def down(h, n, carry):
        j = lax.div(n, 3)
        at = pl.ds(pl.multiple_of(lax.rem(n, 3) * 256, 256), 256)
        out = jnp.dot(act[j, at, :], wd[h, j], preferred_element_type=F32)
        yc[j, at, h * HW : (h + 1) * HW] = out.astype(BF)
        return carry

    def combine(h, s, carry):
        at = pl.ds(pl.multiple_of(s * CAP, 16), CAP)
        outs = jnp.concatenate([yc[j, at, h * HW : (h + 1) * HW] for j in range(SLOTS)], axis=0)
        total = lax.dot_general(pw[s], outs, TN, preferred_element_type=F32).astype(BF)
        for i in range(2):
            part[2 * h + i, s] = total[:, i * QW : (i + 1) * QW]
        return carry

    def ahead(v, h, dirn, k):
        left = h - k
        return wrap(v + left, 4) if dirn == 0 else wrap(v - left, 4)

    def s1_go(q, o, dirn, k):
        a, b, na, nb = axes(q)
        i = hop_index(q, dirn, k)
        target = cid(q, ahead(a, PHOPS[q][dirn], dirn, k), wrap(b + o, 4))
        send(part.at[q, target], rb1.at[q, i, o], r1_s.at[q, i, o], r1_r.at[q, i, o], na[dirn])

    def s2_go(q, dirn, k):
        a, b, na, nb = axes(q)
        i = hop_index(q, dirn, k)
        target = cid(q, a, ahead(b, PHOPS[q][dirn], dirn, k))
        send(part.at[q, target], rb2.at[q, i], r2_s.at[q, i], r2_r.at[q, i], nb[dirn])

    def s1_wait(q, o, dirn, k):
        i = hop_index(q, dirn, k)
        arrived(rb1.at[q, i, o], r1_s.at[q, i, o], r1_r.at[q, i, o])
        return rb1[q, i, o].astype(F32)

    def s2_wait(q, dirn, k):
        i = hop_index(q, dirn, k)
        arrived(rb2.at[q, i], r2_s.at[q, i], r2_r.at[q, i])
        return rb2[q, i].astype(F32)

    def add_into(q, idx, *terms):
        total = part[q, idx].astype(F32)
        for t in terms:
            total = total + t
        part[q, idx] = total.astype(BF)

    offsets = (2, 1, 3, 0)
    own = [None] * 4

    def s1_first(h):
        for o in offsets:
            for q in (2 * h, 2 * h + 1):
                for dirn in range(2):
                    s1_go(q, o, dirn, 0)

    def s1_far(h):
        for o in offsets:
            for q in (2 * h, 2 * h + 1):
                a, b, na, nb = axes(q)
                far = 0 if PHOPS[q][0] == 2 else 1
                add_into(q, cid(q, ahead(a, 2, far, 1), wrap(b + o, 4)), s1_wait(q, o, far, 0))
                s1_go(q, o, far, 1)

    def s1_end(h):
        for o in offsets:
            for q in (2 * h, 2 * h + 1):
                a, b, na, nb = axes(q)
                right, left = PHOPS[q]
                terms = [s1_wait(q, o, 0, right - 1), s1_wait(q, o, 1, left - 1)]
                far = 0 if right == 2 else 1
                mid = 1 if far == 0 else 3
                add_into(q, cid(q, a, wrap(b + o, 4)), *terms)
                if o == 2:
                    s2_go(q, far, 0)
                elif o == 4 - mid:
                    s2_go(q, 1 - far, 0)

    def s2_far(h):
        for q in (2 * h, 2 * h + 1):
            a, b, na, nb = axes(q)
            far = 0 if PHOPS[q][0] == 2 else 1
            add_into(q, cid(q, a, ahead(b, 2, far, 1)), s2_wait(q, far, 0))
            s2_go(q, far, 1)

    def s2_end(h):
        for q in (2 * h, 2 * h + 1):
            right, left = PHOPS[q]
            own[q] = part[q, chip].astype(F32) + s2_wait(q, 0, right - 1) + s2_wait(q, 1, left - 1)

    def produce(h):
        for r in dn[h]:
            r.from_partner()
        lax.fori_loop(0, 12, functools.partial(down, h), 0)
        lax.fori_loop(0, CHIPS, functools.partial(combine, h), 0)
        s1_first(h)
        pump(68)

    produce(0)
    produce(1)
    s1_far(0)
    s1_far(1)
    s1_end(0)
    s2_far(0)
    s1_end(1)
    s2_far(1)
    s2_end(0)
    s2_end(1)
    mixture = jnp.concatenate(own, axis=1)
    out_ref[...] = rms(hid[...].astype(F32) + mixture, fgain[...]).astype(BF)

    for copy in sends:
        copy.wait_send()


def body(
    head_outputs,
    residual,
    output_weight,
    router,
    norm_gain,
    placed_gate_up,
    placed_down,
    routes,
    replica_pick,
    placement,
    final_gain,
):
    dma = pltpu.SemaphoreType.DMA
    anywhere = pl.BlockSpec(memory_space=pl.ANY)
    vmem = pl.BlockSpec(memory_space=pltpu.VMEM)
    return pl.pallas_call(
        body_kernel,
        out_shape=jax.ShapeDtypeStruct((TOK, D), BF),
        in_specs=[anywhere] * 5 + [vmem] * 6,
        out_specs=vmem,
        scratch_shapes=[
            pltpu.VMEM((TOK, D), BF),
            pltpu.VMEM((TOK, D), BF),
            pltpu.VMEM((4, D, QW), BF),
            pltpu.VMEM((2, SLOTS, D, FF), BF),
            pltpu.VMEM((2, SLOTS, FF, HW), BF),
            pltpu.VMEM((4, CHIPS, TOK + 32, QW), BF),
            pltpu.VMEM((SLOTS, ROWS, D), BF),
            pltpu.VMEM((SLOTS, ROWS, FF), BF),
            pltpu.VMEM((SLOTS, ROWS, D), BF),
            pltpu.VMEM((4, CHIPS, TOK, QW), BF),
            pltpu.VMEM((4, 3, 4, TOK, QW), BF),
            pltpu.VMEM((4, 3, TOK, QW), BF),
            pltpu.VMEM((TOK, D), BF),
            pltpu.VMEM((256, TOK), F32),
            pltpu.VMEM((CHIPS, SLOTS * CAP, TOK), BF),
            dma((18,)),
            dma((2, 8)),
            dma((2, 8)),
            dma((2, 8)),
            dma((2, 8)),
            dma((8, 8)),
            dma((8, 8)),
            dma((8, 9)),
            dma((8, 9)),
            dma((4, 3)),
            dma((4, 3)),
            dma((4, 4, 3)),
            dma((4, 4, 3)),
            dma((4, 3, 4)),
            dma((4, 3, 4)),
            dma((4, 3)),
            dma((4, 3)),
        ],
        compiler_params=pltpu.CompilerParams(
            collective_id=0, has_side_effects=True, vmem_limit_bytes=60 * 1024 * 1024
        ),
    )(
        head_outputs,
        residual,
        output_weight,
        placed_gate_up,
        placed_down,
        router,
        norm_gain.reshape(1, D),
        final_gain.reshape(1, D),
        routes,
        replica_pick,
        placement.reshape(1, PL),
    )


def solution(mesh):
    return jax.shard_map(
        body,
        mesh=mesh,
        in_specs=(
            P(("expert", "shard"), None),
            P(("expert", "shard"), None),
            P("shard", None),
            P(),
            P(),
            P("expert", "shard", None),
            P("expert", "shard", None),
            P(("expert", "shard"), None),
            P(("expert", "shard"), None),
            P(),
            P(),
        ),
        out_specs=P(("expert", "shard"), None),
        check_vma=False,
    )
```

```python
import functools

import jax
import jax.numpy as jnp
from jax import lax
from jax.experimental import pallas as pl
from jax.experimental.pallas import tpu as pltpu
from jax.sharding import PartitionSpec as P

NX, NY, NZ = 4, 4, 8
CHIPS = NX * NY
D = 1024
FF = 512
EXPERTS = 32
TOP = 8
TOK = 128
CAP = 48
PL = 64
QW = 256
HW = 512
HALF = FF // 2
SLOTS = 4
ROWS = CHIPS * CAP
EPS = 1e-06
MESH = pl.DeviceIdType.MESH
BF = jnp.bfloat16
F32 = jnp.float32
ZHOPS = ((4, 3), (3, 4))
PHOPS = ((2, 1), (1, 2), (1, 2), (2, 1))
NT = (((1,), (1,)), ((), ()))
TN = (((0,), (0,)), ((), ()))


def wrap(v, n):
    return lax.rem(v + n, n)


def rms(values, gain):
    mean_square = jnp.mean(values * values, axis=-1, keepdims=True)
    return values * lax.rsqrt(mean_square + EPS) * gain


def body_kernel(
    ho,
    res,
    wo_in,
    gu_in,
    dn_in,
    router,
    ngain,
    fgain,
    routes,
    pick,
    plc,
    out_ref,
    ho_v,
    res_v,
    wo,
    wgu,
    wd,
    xq,
    xc,
    act,
    yc,
    part,
    rb1,
    rb2,
    hid,
    pw,
    lsem,
    o_r,
    o_s,
    op_r,
    op_s,
    z_r,
    z_s,
    zp_r,
    zp_s,
    a1_r,
    a1_s,
    a2_r,
    a2_s,
    r1_r,
    r1_s,
    r2_r,
    r2_s,
):
    e = lax.axis_index("expert")
    z = lax.axis_index("shard")
    chip = lax.div(e, 2)
    core = lax.rem(e, 2)
    x = lax.div(chip, NY)
    y = lax.rem(chip, NY)

    def dev(xx, yy, zz, cc):
        return ((xx * NY + yy) * 2 + cc, zz)

    partner = dev(x, y, z, 1 - core)
    znb = (dev(x, y, wrap(z + 1, NZ), core), dev(x, y, wrap(z - 1, NZ), core))
    xnb = (dev(wrap(x + 1, NX), y, z, core), dev(wrap(x - 1, NX), y, z, core))
    ynb = (dev(x, wrap(y + 1, NY), z, core), dev(x, wrap(y - 1, NY), z, core))

    sends = []

    def send(src, dst, ssem, rsem, to):
        copy = pltpu.make_async_remote_copy(
            src_ref=src, dst_ref=dst, send_sem=ssem, recv_sem=rsem, device_id=to, device_id_type=MESH
        )
        copy.start()
        sends.append(copy)

    def arrived(dst, ssem, rsem):
        pltpu.make_async_remote_copy(
            src_ref=dst, dst_ref=dst, send_sem=ssem, recv_sem=rsem, device_id=partner, device_id_type=MESH
        ).wait_recv()

    zrow = pl.ds(pl.multiple_of(z * 128, 128), 128)
    zrow2 = pl.ds(pl.multiple_of(z * 64, 64), 64)
    local = []

    def load(src, dst):
        copy = pltpu.make_async_copy(src, dst, lsem.at[len(local)])
        copy.start()
        local.append(copy)

    for q in range(4):
        load(wo_in.at[:, pl.ds(q * QW, QW)], wo.at[q, zrow, :])
    load(ho, ho_v)
    load(res, res_v)
    for c in range(2):
        for j in range(2):
            s = 2 * core + j
            load(gu_in.at[j, :, pl.ds(c * HALF, HALF)], wgu.at[c, s, zrow, pl.ds(0, HALF)])
            load(gu_in.at[j, :, pl.ds(FF + c * HALF, HALF)], wgu.at[c, s, zrow, pl.ds(HALF, HALF)])
    for h in range(2):
        for j in range(2):
            load(dn_in.at[j, :, pl.ds(h * HW, HW)], wd.at[h, 2 * core + j, zrow2, :])

    barrier = pltpu.get_barrier_semaphore()
    for nb in (partner,) + znb + xnb + ynb:
        pl.semaphore_signal(barrier, inc=1, device_id=nb, device_id_type=MESH)
    pl.semaphore_wait(barrier, 7)

    for copy in local:
        copy.wait()

    def shard_of(dirn, k):
        return wrap(z - k, NZ) if dirn == 0 else wrap(z + k, NZ)

    class Ring:
        def __init__(self, where, hops, s_sem, r_sem, ps_sem, pr_sem, share_own):
            self.where, self.hops = where, hops
            self.s_sem, self.r_sem, self.ps_sem, self.pr_sem = s_sem, r_sem, ps_sem, pr_sem
            self.share_own = share_own

        def go(self, dirn, k):
            at = self.where(core, shard_of(dirn, k))
            i = dirn * 4 + k
            send(at, at, self.s_sem(i), self.r_sem(i), znb[dirn])

        def begin(self):
            self.go(0, 0)
            self.go(1, 0)
            if self.share_own:
                at = self.where(core, z)
                send(at, at, self.ps_sem(8), self.pr_sem(8), partner)

        def arrive(self, k):
            for dirn in range(2):
                if k < self.hops[dirn]:
                    i = dirn * 4 + k
                    at = self.where(core, shard_of(dirn, k + 1))
                    arrived(at, self.s_sem(i), self.r_sem(i))
                    if k + 1 < self.hops[dirn]:
                        self.go(dirn, k + 1)
                    send(at, at, self.ps_sem(i), self.pr_sem(i), partner)

        def from_partner(self):
            other = 1 - core
            for dirn in range(2):
                for k in range(self.hops[dirn]):
                    i = dirn * 4 + k
                    arrived(self.where(other, shard_of(dirn, k + 1)), self.ps_sem(i), self.pr_sem(i))
            if self.share_own:
                arrived(self.where(other, z), self.ps_sem(8), self.pr_sem(8))

    def wo_at(i):
        return lambda cc, zz: wo.at[2 * cc + i, pl.ds(pl.multiple_of(zz * 128, 128), 128), :]

    def gu_at(c, j):
        return lambda cc, zz: wgu.at[c, 2 * cc + j, pl.ds(pl.multiple_of(zz * 128, 128), 128), :]

    def dn_at(h, j):
        return lambda cc, zz: wd.at[h, 2 * cc + j, pl.ds(pl.multiple_of(zz * 64, 64), 64), :]

    def sem_row(ref, u):
        return lambda i: ref.at[u, i]

    def ring(where, u, hops, refs, own):
        return Ring(where, hops, *[sem_row(r, u) for r in refs], own)

    orings = [ring(wo_at(i), i, ZHOPS[i], (o_s, o_r, op_s, op_r), False) for i in range(2)]
    zrefs = (z_s, z_r, zp_s, zp_r)
    gu = [[ring(gu_at(c, j), 2 * c + j, ZHOPS[j], zrefs, True) for j in range(2)] for c in range(2)]
    dn = [[ring(dn_at(h, j), 4 + 2 * h + j, ZHOPS[j], zrefs, True) for j in range(2)] for h in range(2)]

    zqueue = [
        (21, gu[0], 0),
        (27, gu[1], 0),
        (32, gu[0], 1),
        (38, gu[1], 1),
        (44, gu[0], 2),
        (45, dn[0], 0),
        (49, gu[1], 2),
        (52, dn[0], 1),
        (53, dn[1], 0),
        (54, gu[0], 3),
        (57, dn[0], 2),
        (58, gu[1], 3),
        (60, dn[1], 1),
        (62, dn[0], 3),
        (64, dn[1], 2),
        (68, dn[1], 3),
    ]

    def pump(now):
        while zqueue and zqueue[0][0] <= now:
            _, rings, k = zqueue.pop(0)
            for r in rings:
                r.arrive(k)

    for r in orings:
        r.begin()
    dn[0][0].begin()
    for k in range(3):
        for r in orings:
            r.arrive(k)
        (dn[0][1], dn[1][0], dn[1][1])[k].begin()
    for r in gu[0] + gu[1]:
        r.begin()

    plc_row = plc[...].astype(F32)
    rows64 = lax.broadcasted_iota(jnp.int32, (PL, PL), 0)
    cols64 = lax.broadcasted_iota(jnp.int32, (PL, PL), 1)
    plc_col = jnp.sum(jnp.where(rows64 == cols64, plc_row, 0.0), axis=1, keepdims=True)
    same = plc_col == plc_row
    copies = jnp.sum(jnp.where(same, 1.0, 0.0), axis=1, keepdims=True)
    order = jnp.sum(jnp.where(same & (cols64 < rows64), 1.0, 0.0), axis=1, keepdims=True)
    routes_t = routes[...].astype(F32)
    pick_t = pick[...].astype(F32)
    hit = jnp.zeros((PL, TOK), F32)
    for k in range(TOP):
        route = routes_t[k : k + 1, :]
        p = pick_t[k : k + 1, :]
        by2 = p - jnp.where(p >= 2.0, 2.0, 0.0) - jnp.where(p >= 4.0, 2.0, 0.0)
        by3 = p - jnp.where(p >= 3.0, 3.0, 0.0)
        wanted = jnp.where(copies == 1.0, 0.0, jnp.where(copies == 2.0, by2, by3))
        hit = hit + jnp.where((route == plc_col) & (wanted == order), 1.0, 0.0)
    names = (plc_col == lax.broadcasted_iota(jnp.int32, (PL, EXPERTS), 1).astype(F32)).astype(BF)
    router_rows = jnp.dot(names, router[...], preferred_element_type=F32).astype(BF)

    for r in orings:
        r.arrive(3)
    for r in orings:
        r.from_partner()

    for q in range(4):
        cols = pl.ds(q * QW, QW)
        projected = jnp.dot(ho_v[...], wo[q], preferred_element_type=F32)
        hid[:, cols] = (res_v[:, cols].astype(F32) + projected).astype(BF)
    normed = rms(hid[...].astype(F32), ngain[...]).astype(BF)
    logits = lax.dot_general(router_rows, normed, NT, preferred_element_type=F32)
    raised = jnp.where(hit > 0.0, jnp.exp(logits), 0.0)
    weight = (raised / jnp.sum(raised, axis=0, keepdims=True)).astype(BF)
    for q in range(4):
        xq[q, chip, 0:TOK, :] = normed[:, q * QW : (q + 1) * QW]
    xq[0, chip, TOK : TOK + 32, 0:128] = weight[0:32, :]
    xq[0, chip, TOK : TOK + 32, 128:256] = weight[32:64, :]

    def axes(q):
        return (x, y, xnb, ynb) if q % 2 == 0 else (y, x, ynb, xnb)

    def cid(q, aa, bb):
        return aa * NY + bb if q % 2 == 0 else bb * NY + aa

    def block(q, idx):
        return xq.at[q, idx, pl.ds(0, TOK + 32 if q == 0 else TOK), :]

    def back(v, dirn, k):
        return wrap(v - k, 4) if dirn == 0 else wrap(v + k, 4)

    def hop_index(q, dirn, k):
        return k if dirn == 0 else PHOPS[q][0] + k

    def a1_go(q, dirn, k):
        a, b, na, nb = axes(q)
        at = block(q, cid(q, back(a, dirn, k), b))
        i = hop_index(q, dirn, k)
        send(at, at, a1_s.at[q, i], a1_r.at[q, i], na[dirn])

    def a2_go(q, label, aa, dirn, k):
        a, b, na, nb = axes(q)
        at = block(q, cid(q, aa, back(b, dirn, k)))
        i = hop_index(q, dirn, k)
        send(at, at, a2_s.at[q, label, i], a2_r.at[q, label, i], nb[dirn])

    def a1_arrive(q, dirn, k):
        a, b, na, nb = axes(q)
        aa = back(a, dirn, k + 1)
        i = hop_index(q, dirn, k)
        arrived(block(q, cid(q, aa, b)), a1_s.at[q, i], a1_r.at[q, i])
        if k + 1 < PHOPS[q][dirn]:
            a1_go(q, dirn, k + 1)
        for d2 in range(2):
            a2_go(q, 1 + i, aa, d2, 0)

    def a2_arrive(q, label, aa, dirn, k):
        a, b, na, nb = axes(q)
        i = hop_index(q, dirn, k)
        arrived(block(q, cid(q, aa, back(b, dirn, k + 1))), a2_s.at[q, label, i], a2_r.at[q, label, i])
        if k + 1 < PHOPS[q][dirn]:
            a2_go(q, label, aa, dirn, k + 1)

    for q in range(4):
        a = axes(q)[0]
        for dirn in range(2):
            a1_go(q, dirn, 0)
        for dirn in range(2):
            a2_go(q, 0, a, dirn, 0)
    events = []
    for q in range(4):
        a = axes(q)[0]
        hops = [(dirn, k) for dirn in range(2) for k in range(PHOPS[q][dirn])]
        for d2, k2 in hops:
            events.append((k2 + 1, q, functools.partial(a2_arrive, q, 0, a, d2, k2)))
        for dirn, k in hops:
            events.append((k + 1, q, functools.partial(a1_arrive, q, dirn, k)))
            aa = back(a, dirn, k + 1)
            label = 1 + hop_index(q, dirn, k)
            for d2, k2 in hops:
                events.append((k + k2 + 2, q, functools.partial(a2_arrive, q, label, aa, d2, k2)))
    events.sort(key=lambda ev: ev[:2])

    lane32 = lax.broadcasted_iota(jnp.int32, (TOP, 32), 1)
    row32 = lax.broadcasted_iota(jnp.int32, (TOP, 32), 0)
    mine = SLOTS * chip + row32
    pick_lo = ((lane32 == mine) & (row32 < SLOTS)).astype(BF)
    pick_hi = ((lane32 + 32 == mine) & (row32 < SLOTS)).astype(BF)
    rows128 = lax.broadcasted_iota(jnp.int32, (TOK, TOK), 0)
    cols128 = lax.broadcasted_iota(jnp.int32, (TOK, TOK), 1)
    earlier = (rows128 < cols128).astype(BF)

    def compact(where, n, carry):
        dx, dy = where(lax.div(n, 2), lax.rem(n, 2))
        s = wrap(x + dx, NX) * NY + wrap(y + dy, NY)
        table = xq[0, s, TOK : TOK + 32, :]
        w8 = jnp.dot(pick_lo, table[:, 0:128], preferred_element_type=F32) + jnp.dot(
            pick_hi, table[:, 128:256], preferred_element_type=F32
        )
        taken = w8 > 0.0
        rank = jnp.dot(jnp.where(taken, 1.0, 0.0).astype(BF), earlier, preferred_element_type=F32)
        r8 = jnp.where(taken, rank, -1.0)
        rows = lax.broadcasted_iota(jnp.int32, (CAP, TOK), 0).astype(F32)
        here = [rows == r8[j : j + 1, :] for j in range(SLOTS)]
        chosen = jnp.concatenate([jnp.where(h, 1.0, 0.0) for h in here], axis=0).astype(BF)
        pw[s] = jnp.concatenate(
            [jnp.where(here[j], w8[j : j + 1, :], 0.0) for j in range(SLOTS)], axis=0
        ).astype(BF)
        tokens = jnp.concatenate([xq[q, s, 0:TOK, :] for q in range(4)], axis=1)
        packed = jnp.dot(chosen, tokens, preferred_element_type=F32).astype(BF)
        for j in range(SLOTS):
            xc[j, pl.ds(pl.multiple_of(s * CAP, 16), CAP), :] = packed[j * CAP : (j + 1) * CAP, :]
        return carry

    def compact_some(count, where):
        lax.fori_loop(0, count, functools.partial(compact, where), 0)

    ready = {
        8: ((1, lambda h, m: (h, m)),),
        24: ((4, lambda h, m: ((1 - h) * (1 + 2 * m), h * (1 + 2 * m))),),
        44: ((2, lambda h, m: (2 * m, 2 - 2 * m)), (4, lambda h, m: (1 + 2 * h, 1 + 2 * m))),
        58: ((4, lambda h, m: ((1 - h) * (1 + 2 * m) + 2 * h, h * (1 + 2 * m) + 2 - 2 * h)),),
    }
    for n, (_, _, run) in enumerate(events):
        pump(22.5 + 0.38 * n)
        run()
        for group in ready.get(n, ()):
            compact_some(*group)
    pump(45)
    compact_some(1, lambda h, m: (2 + h, 2 + m))
    pump(53)

    def gate_up(c, n, carry):
        j = lax.div(n, 3)
        at = pl.ds(pl.multiple_of(lax.rem(n, 3) * 256, 256), 256)
        both = jnp.dot(xc[j, at, :], wgu[c, j], preferred_element_type=F32)
        g, u = both[:, 0:HALF], both[:, HALF:]
        act[j, at, c * HALF : (c + 1) * HALF] = (g / (1.0 + jnp.exp(-g)) * u).astype(BF)
        return carry

    pump(54)
    for r in gu[0]:
        r.from_partner()
    for g in range(2):
        lax.fori_loop(g * 6, g * 6 + 6, functools.partial(gate_up, 0), 0)
        pump((57, 60)[g])
    for r in gu[1]:
        r.from_partner()
    for g in range(2):
        lax.fori_loop(g * 6, g * 6 + 6, functools.partial(gate_up, 1), 0)
        pump((62, 64)[g])

    def down(h, n, carry):
        j = lax.div(n, 3)
        at = pl.ds(pl.multiple_of(lax.rem(n, 3) * 256, 256), 256)
        out = jnp.dot(act[j, at, :], wd[h, j], preferred_element_type=F32)
        yc[j, at, h * HW : (h + 1) * HW] = out.astype(BF)
        return carry

    def combine(h, s, carry):
        at = pl.ds(pl.multiple_of(s * CAP, 16), CAP)
        outs = jnp.concatenate([yc[j, at, h * HW : (h + 1) * HW] for j in range(SLOTS)], axis=0)
        total = lax.dot_general(pw[s], outs, TN, preferred_element_type=F32).astype(BF)
        for i in range(2):
            part[2 * h + i, s] = total[:, i * QW : (i + 1) * QW]
        return carry

    def ahead(v, h, dirn, k):
        left = h - k
        return wrap(v + left, 4) if dirn == 0 else wrap(v - left, 4)

    def s1_go(q, o, dirn, k):
        a, b, na, nb = axes(q)
        i = hop_index(q, dirn, k)
        target = cid(q, ahead(a, PHOPS[q][dirn], dirn, k), wrap(b + o, 4))
        send(part.at[q, target], rb1.at[q, i, o], r1_s.at[q, i, o], r1_r.at[q, i, o], na[dirn])

    def s2_go(q, dirn, k):
        a, b, na, nb = axes(q)
        i = hop_index(q, dirn, k)
        target = cid(q, a, ahead(b, PHOPS[q][dirn], dirn, k))
        send(part.at[q, target], rb2.at[q, i], r2_s.at[q, i], r2_r.at[q, i], nb[dirn])

    def s1_wait(q, o, dirn, k):
        i = hop_index(q, dirn, k)
        arrived(rb1.at[q, i, o], r1_s.at[q, i, o], r1_r.at[q, i, o])
        return rb1[q, i, o].astype(F32)

    def s2_wait(q, dirn, k):
        i = hop_index(q, dirn, k)
        arrived(rb2.at[q, i], r2_s.at[q, i], r2_r.at[q, i])
        return rb2[q, i].astype(F32)

    def add_into(q, idx, *terms):
        total = part[q, idx].astype(F32)
        for t in terms:
            total = total + t
        part[q, idx] = total.astype(BF)

    offsets = (2, 1, 3, 0)
    own = [None] * 4

    def s1_first(h):
        for o in offsets:
            for q in (2 * h, 2 * h + 1):
                for dirn in range(2):
                    s1_go(q, o, dirn, 0)

    def s1_far(h):
        for o in offsets:
            for q in (2 * h, 2 * h + 1):
                a, b, na, nb = axes(q)
                far = 0 if PHOPS[q][0] == 2 else 1
                add_into(q, cid(q, ahead(a, 2, far, 1), wrap(b + o, 4)), s1_wait(q, o, far, 0))
                s1_go(q, o, far, 1)

    def s1_end(h):
        for o in offsets:
            for q in (2 * h, 2 * h + 1):
                a, b, na, nb = axes(q)
                right, left = PHOPS[q]
                terms = [s1_wait(q, o, 0, right - 1), s1_wait(q, o, 1, left - 1)]
                far = 0 if right == 2 else 1
                mid = 1 if far == 0 else 3
                add_into(q, cid(q, a, wrap(b + o, 4)), *terms)
                if o == 2:
                    s2_go(q, far, 0)
                elif o == 4 - mid:
                    s2_go(q, 1 - far, 0)

    def s2_far(h):
        for q in (2 * h, 2 * h + 1):
            a, b, na, nb = axes(q)
            far = 0 if PHOPS[q][0] == 2 else 1
            add_into(q, cid(q, a, ahead(b, 2, far, 1)), s2_wait(q, far, 0))
            s2_go(q, far, 1)

    def s2_end(h):
        for q in (2 * h, 2 * h + 1):
            right, left = PHOPS[q]
            own[q] = part[q, chip].astype(F32) + s2_wait(q, 0, right - 1) + s2_wait(q, 1, left - 1)

    def produce(h):
        for r in dn[h]:
            r.from_partner()
        lax.fori_loop(0, 12, functools.partial(down, h), 0)
        lax.fori_loop(0, CHIPS, functools.partial(combine, h), 0)
        s1_first(h)
        pump(68)

    produce(0)
    produce(1)
    s1_far(0)
    s1_far(1)
    s1_end(0)
    s2_far(0)
    s1_end(1)
    s2_far(1)
    s2_end(0)
    s2_end(1)
    mixture = jnp.concatenate(own, axis=1)
    out_ref[...] = rms(hid[...].astype(F32) + mixture, fgain[...]).astype(BF)

    for copy in sends:
        copy.wait_send()


def body(
    head_outputs,
    residual,
    output_weight,
    router,
    norm_gain,
    placed_gate_up,
    placed_down,
    routes,
    replica_pick,
    placement,
    final_gain,
):
    dma = pltpu.SemaphoreType.DMA
    anywhere = pl.BlockSpec(memory_space=pl.ANY)
    vmem = pl.BlockSpec(memory_space=pltpu.VMEM)
    return pl.pallas_call(
        body_kernel,
        out_shape=jax.ShapeDtypeStruct((TOK, D), BF),
        in_specs=[anywhere] * 5 + [vmem] * 6,
        out_specs=vmem,
        scratch_shapes=[
            pltpu.VMEM((TOK, D), BF),
            pltpu.VMEM((TOK, D), BF),
            pltpu.VMEM((4, D, QW), BF),
            pltpu.VMEM((2, SLOTS, D, FF), BF),
            pltpu.VMEM((2, SLOTS, FF, HW), BF),
            pltpu.VMEM((4, CHIPS, TOK + 32, QW), BF),
            pltpu.VMEM((SLOTS, ROWS, D), BF),
            pltpu.VMEM((SLOTS, ROWS, FF), BF),
            pltpu.VMEM((SLOTS, ROWS, D), BF),
            pltpu.VMEM((4, CHIPS, TOK, QW), BF),
            pltpu.VMEM((4, 3, 4, TOK, QW), BF),
            pltpu.VMEM((4, 3, TOK, QW), BF),
            pltpu.VMEM((TOK, D), BF),
            pltpu.VMEM((CHIPS, SLOTS * CAP, TOK), BF),
            dma((18,)),
            dma((2, 8)),
            dma((2, 8)),
            dma((2, 8)),
            dma((2, 8)),
            dma((8, 8)),
            dma((8, 8)),
            dma((8, 9)),
            dma((8, 9)),
            dma((4, 3)),
            dma((4, 3)),
            dma((4, 4, 3)),
            dma((4, 4, 3)),
            dma((4, 3, 4)),
            dma((4, 3, 4)),
            dma((4, 3)),
            dma((4, 3)),
        ],
        compiler_params=pltpu.CompilerParams(
            collective_id=0, has_side_effects=True, vmem_limit_bytes=60 * 1024 * 1024
        ),
    )(
        head_outputs,
        residual,
        output_weight,
        placed_gate_up,
        placed_down,
        router.T,
        norm_gain.reshape(1, D),
        final_gain.reshape(1, D),
        routes.T,
        replica_pick.T,
        placement.reshape(1, PL),
    )


def solution(mesh):
    return jax.shard_map(
        body,
        mesh=mesh,
        in_specs=(
            P(("expert", "shard"), None),
            P(("expert", "shard"), None),
            P("shard", None),
            P(),
            P(),
            P("expert", "shard", None),
            P("expert", "shard", None),
            P(("expert", "shard"), None),
            P(("expert", "shard"), None),
            P(),
            P(),
        ),
        out_specs=P(("expert", "shard"), None),
        check_vma=False,
    )
```

```python
import functools

import jax
import jax.numpy as jnp
from jax import lax
from jax.experimental import pallas as pl
from jax.experimental.pallas import tpu as pltpu
from jax.sharding import PartitionSpec as P

NX, NY, NZ = 4, 4, 8
CHIPS = NX * NY
D = 1024
FF = 512
EXPERTS = 32
TOP = 8
TOK = 128
CAP = 48
PL = 64
QW = 256
HW = 512
HALF = FF // 2
SLOTS = 4
ROWS = CHIPS * CAP
EPS = 1e-06
MESH = pl.DeviceIdType.MESH
BF = jnp.bfloat16
F32 = jnp.float32
ZHOPS = ((4, 3), (3, 4))
PHOPS = ((2, 1), (1, 2), (1, 2), (2, 1))
NT = (((1,), (1,)), ((), ()))
TN = (((0,), (0,)), ((), ()))


def wrap(v, n):
    return lax.rem(v + n, n)


def rms(values, gain):
    mean_square = jnp.mean(values * values, axis=-1, keepdims=True)
    return values * lax.rsqrt(mean_square + EPS) * gain


def body_kernel(
    ho,
    res,
    wo_in,
    gu_in,
    dn_in,
    router,
    ngain,
    fgain,
    routes,
    pick,
    plc,
    out_ref,
    ho_v,
    res_v,
    wo,
    wgu,
    wd,
    xq,
    xc,
    act,
    yc,
    part,
    rb1,
    rb2,
    hid,
    pw,
    lsem,
    o_r,
    o_s,
    op_r,
    op_s,
    z_r,
    z_s,
    zp_r,
    zp_s,
    a1_r,
    a1_s,
    a2_r,
    a2_s,
    r1_r,
    r1_s,
    r2_r,
    r2_s,
):
    e = lax.axis_index("expert")
    z = lax.axis_index("shard")
    chip = lax.div(e, 2)
    core = lax.rem(e, 2)
    x = lax.div(chip, NY)
    y = lax.rem(chip, NY)

    def dev(xx, yy, zz, cc):
        return ((xx * NY + yy) * 2 + cc, zz)

    partner = dev(x, y, z, 1 - core)
    znb = (dev(x, y, wrap(z + 1, NZ), core), dev(x, y, wrap(z - 1, NZ), core))
    xnb = (dev(wrap(x + 1, NX), y, z, core), dev(wrap(x - 1, NX), y, z, core))
    ynb = (dev(x, wrap(y + 1, NY), z, core), dev(x, wrap(y - 1, NY), z, core))

    sends = []

    def send(src, dst, ssem, rsem, to):
        copy = pltpu.make_async_remote_copy(
            src_ref=src, dst_ref=dst, send_sem=ssem, recv_sem=rsem, device_id=to, device_id_type=MESH
        )
        copy.start()
        sends.append(copy)

    def arrived(dst, ssem, rsem):
        pltpu.make_async_remote_copy(
            src_ref=dst, dst_ref=dst, send_sem=ssem, recv_sem=rsem, device_id=partner, device_id_type=MESH
        ).wait_recv()

    zrow = pl.ds(pl.multiple_of(z * 128, 128), 128)
    zrow2 = pl.ds(pl.multiple_of(z * 64, 64), 64)
    local = []

    def load(src, dst):
        copy = pltpu.make_async_copy(src, dst, lsem.at[len(local)])
        copy.start()
        local.append(copy)

    for q in range(4):
        load(wo_in.at[:, pl.ds(q * QW, QW)], wo.at[q, zrow, :])
    load(ho, ho_v)
    load(res, res_v)
    for c in range(2):
        for j in range(2):
            s = 2 * core + j
            load(gu_in.at[j, :, pl.ds(c * HALF, HALF)], wgu.at[c, s, zrow, pl.ds(0, HALF)])
            load(gu_in.at[j, :, pl.ds(FF + c * HALF, HALF)], wgu.at[c, s, zrow, pl.ds(HALF, HALF)])
    for h in range(2):
        for j in range(2):
            load(dn_in.at[j, :, pl.ds(h * HW, HW)], wd.at[h, 2 * core + j, zrow2, :])

    barrier = pltpu.get_barrier_semaphore()
    for nb in (partner,) + znb + xnb + ynb:
        pl.semaphore_signal(barrier, inc=1, device_id=nb, device_id_type=MESH)
    pl.semaphore_wait(barrier, 7)

    for copy in local:
        copy.wait()

    def shard_of(dirn, k):
        return wrap(z - k, NZ) if dirn == 0 else wrap(z + k, NZ)

    class Ring:
        def __init__(self, where, hops, s_sem, r_sem, ps_sem, pr_sem, share_own):
            self.where, self.hops = where, hops
            self.s_sem, self.r_sem, self.ps_sem, self.pr_sem = s_sem, r_sem, ps_sem, pr_sem
            self.share_own = share_own

        def go(self, dirn, k):
            at = self.where(core, shard_of(dirn, k))
            i = dirn * 4 + k
            send(at, at, self.s_sem(i), self.r_sem(i), znb[dirn])

        def begin(self):
            self.go(0, 0)
            self.go(1, 0)
            if self.share_own:
                at = self.where(core, z)
                send(at, at, self.ps_sem(8), self.pr_sem(8), partner)

        def arrive(self, k):
            for dirn in range(2):
                if k < self.hops[dirn]:
                    i = dirn * 4 + k
                    at = self.where(core, shard_of(dirn, k + 1))
                    arrived(at, self.s_sem(i), self.r_sem(i))
                    if k + 1 < self.hops[dirn]:
                        self.go(dirn, k + 1)
                    send(at, at, self.ps_sem(i), self.pr_sem(i), partner)

        def from_partner(self):
            other = 1 - core
            for dirn in range(2):
                for k in range(self.hops[dirn]):
                    i = dirn * 4 + k
                    arrived(self.where(other, shard_of(dirn, k + 1)), self.ps_sem(i), self.pr_sem(i))
            if self.share_own:
                arrived(self.where(other, z), self.ps_sem(8), self.pr_sem(8))

    def wo_at(i):
        return lambda cc, zz: wo.at[2 * cc + i, pl.ds(pl.multiple_of(zz * 128, 128), 128), :]

    def gu_at(c, j):
        return lambda cc, zz: wgu.at[c, 2 * cc + j, pl.ds(pl.multiple_of(zz * 128, 128), 128), :]

    def dn_at(h, j):
        return lambda cc, zz: wd.at[h, 2 * cc + j, pl.ds(pl.multiple_of(zz * 64, 64), 64), :]

    def sem_row(ref, u):
        return lambda i: ref.at[u, i]

    def ring(where, u, hops, refs, own):
        return Ring(where, hops, *[sem_row(r, u) for r in refs], own)

    orings = [ring(wo_at(i), i, ZHOPS[i], (o_s, o_r, op_s, op_r), False) for i in range(2)]
    zrefs = (z_s, z_r, zp_s, zp_r)
    gu = [[ring(gu_at(c, j), 2 * c + j, ZHOPS[j], zrefs, True) for j in range(2)] for c in range(2)]
    dn = [[ring(dn_at(h, j), 4 + 2 * h + j, ZHOPS[j], zrefs, True) for j in range(2)] for h in range(2)]

    zqueue = [
        (21, gu[0], 0),
        (27, gu[1], 0),
        (32, gu[0], 1),
        (38, gu[1], 1),
        (44, gu[0], 2),
        (45, dn[0], 0),
        (49, gu[1], 2),
        (52, dn[0], 1),
        (53, dn[1], 0),
        (54, gu[0], 3),
        (57, dn[0], 2),
        (58, gu[1], 3),
        (60, dn[1], 1),
        (62, dn[0], 3),
        (64, dn[1], 2),
        (68, dn[1], 3),
    ]

    def pump(now):
        while zqueue and zqueue[0][0] <= now:
            _, rings, k = zqueue.pop(0)
            for r in rings:
                r.arrive(k)

    for r in orings:
        r.begin()
    dn[0][0].begin()
    for k in range(3):
        for r in orings:
            r.arrive(k)
        (dn[0][1], dn[1][0], dn[1][1])[k].begin()
    for r in gu[0] + gu[1]:
        r.begin()

    plc_row = plc[...].astype(F32)
    rows64 = lax.broadcasted_iota(jnp.int32, (PL, PL), 0)
    cols64 = lax.broadcasted_iota(jnp.int32, (PL, PL), 1)
    plc_col = jnp.sum(jnp.where(rows64 == cols64, plc_row, 0.0), axis=1, keepdims=True)
    same = plc_col == plc_row
    copies = jnp.sum(jnp.where(same, 1.0, 0.0), axis=1, keepdims=True)
    order = jnp.sum(jnp.where(same & (cols64 < rows64), 1.0, 0.0), axis=1, keepdims=True)
    routes_t = routes[...].astype(F32)
    pick_t = pick[...].astype(F32)
    hit = jnp.zeros((PL, TOK), F32)
    for k in range(TOP):
        route = routes_t[k : k + 1, :]
        p = pick_t[k : k + 1, :]
        by2 = p - jnp.where(p >= 2.0, 2.0, 0.0) - jnp.where(p >= 4.0, 2.0, 0.0)
        by3 = p - jnp.where(p >= 3.0, 3.0, 0.0)
        wanted = jnp.where(copies == 1.0, 0.0, jnp.where(copies == 2.0, by2, by3))
        hit = hit + jnp.where((route == plc_col) & (wanted == order), 1.0, 0.0)
    names = (plc_col == lax.broadcasted_iota(jnp.int32, (PL, EXPERTS), 1).astype(F32)).astype(BF)
    router_rows = jnp.dot(names, router[...], preferred_element_type=F32).astype(BF)

    for r in orings:
        r.arrive(3)
    for r in orings:
        r.from_partner()

    for q in range(4):
        cols = pl.ds(q * QW, QW)
        projected = jnp.dot(ho_v[...], wo[q], preferred_element_type=F32)
        hid[:, cols] = (res_v[:, cols].astype(F32) + projected).astype(BF)
    normed = rms(hid[...].astype(F32), ngain[...]).astype(BF)
    logits = lax.dot_general(router_rows, normed, NT, preferred_element_type=F32)
    raised = jnp.where(hit > 0.0, jnp.exp(logits), 0.0)
    weight = (raised / jnp.sum(raised, axis=0, keepdims=True)).astype(BF)
    for q in range(4):
        xq[q, chip, 0:TOK, :] = normed[:, q * QW : (q + 1) * QW]
    xq[0, chip, TOK : TOK + 32, 0:128] = weight[0:32, :]
    xq[0, chip, TOK : TOK + 32, 128:256] = weight[32:64, :]

    def axes(q):
        return (x, y, xnb, ynb) if q % 2 == 0 else (y, x, ynb, xnb)

    def cid(q, aa, bb):
        return aa * NY + bb if q % 2 == 0 else bb * NY + aa

    def block(q, idx):
        return xq.at[q, idx, pl.ds(0, TOK + 32 if q == 0 else TOK), :]

    def back(v, dirn, k):
        return wrap(v - k, 4) if dirn == 0 else wrap(v + k, 4)

    def hop_index(q, dirn, k):
        return k if dirn == 0 else PHOPS[q][0] + k

    def a1_go(q, dirn, k):
        a, b, na, nb = axes(q)
        at = block(q, cid(q, back(a, dirn, k), b))
        i = hop_index(q, dirn, k)
        send(at, at, a1_s.at[q, i], a1_r.at[q, i], na[dirn])

    def a2_go(q, label, aa, dirn, k):
        a, b, na, nb = axes(q)
        at = block(q, cid(q, aa, back(b, dirn, k)))
        i = hop_index(q, dirn, k)
        send(at, at, a2_s.at[q, label, i], a2_r.at[q, label, i], nb[dirn])

    def a1_arrive(q, dirn, k):
        a, b, na, nb = axes(q)
        aa = back(a, dirn, k + 1)
        i = hop_index(q, dirn, k)
        arrived(block(q, cid(q, aa, b)), a1_s.at[q, i], a1_r.at[q, i])
        if k + 1 < PHOPS[q][dirn]:
            a1_go(q, dirn, k + 1)
        for d2 in range(2):
            a2_go(q, 1 + i, aa, d2, 0)

    def a2_arrive(q, label, aa, dirn, k):
        a, b, na, nb = axes(q)
        i = hop_index(q, dirn, k)
        arrived(block(q, cid(q, aa, back(b, dirn, k + 1))), a2_s.at[q, label, i], a2_r.at[q, label, i])
        if k + 1 < PHOPS[q][dirn]:
            a2_go(q, label, aa, dirn, k + 1)

    for q in range(4):
        a = axes(q)[0]
        for dirn in range(2):
            a1_go(q, dirn, 0)
        for dirn in range(2):
            a2_go(q, 0, a, dirn, 0)
    events = []
    for q in range(4):
        a = axes(q)[0]
        hops = [(dirn, k) for dirn in range(2) for k in range(PHOPS[q][dirn])]
        for d2, k2 in hops:
            events.append((k2 + 1, q, functools.partial(a2_arrive, q, 0, a, d2, k2)))
        for dirn, k in hops:
            events.append((k + 1, q, functools.partial(a1_arrive, q, dirn, k)))
            aa = back(a, dirn, k + 1)
            label = 1 + hop_index(q, dirn, k)
            for d2, k2 in hops:
                events.append((k + k2 + 2, q, functools.partial(a2_arrive, q, label, aa, d2, k2)))
    events.sort(key=lambda ev: ev[:2])

    lane32 = lax.broadcasted_iota(jnp.int32, (TOP, 32), 1)
    row32 = lax.broadcasted_iota(jnp.int32, (TOP, 32), 0)
    mine = SLOTS * chip + row32
    pick_lo = ((lane32 == mine) & (row32 < SLOTS)).astype(BF)
    pick_hi = ((lane32 + 32 == mine) & (row32 < SLOTS)).astype(BF)
    rows128 = lax.broadcasted_iota(jnp.int32, (TOK, TOK), 0)
    cols128 = lax.broadcasted_iota(jnp.int32, (TOK, TOK), 1)
    earlier = (rows128 < cols128).astype(BF)

    def compact(where, n, carry):
        dx, dy = where(lax.div(n, 2), lax.rem(n, 2))
        s = wrap(x + dx, NX) * NY + wrap(y + dy, NY)
        table = xq[0, s, TOK : TOK + 32, :]
        w8 = jnp.dot(pick_lo, table[:, 0:128], preferred_element_type=F32) + jnp.dot(
            pick_hi, table[:, 128:256], preferred_element_type=F32
        )
        taken = w8 > 0.0
        rank = jnp.dot(jnp.where(taken, 1.0, 0.0).astype(BF), earlier, preferred_element_type=F32)
        r8 = jnp.where(taken, rank, -1.0)
        rows = lax.broadcasted_iota(jnp.int32, (CAP, TOK), 0).astype(F32)
        here = [rows == r8[j : j + 1, :] for j in range(SLOTS)]
        chosen = jnp.concatenate([jnp.where(h, 1.0, 0.0) for h in here], axis=0).astype(BF)
        pw[s] = jnp.concatenate(
            [jnp.where(here[j], w8[j : j + 1, :], 0.0) for j in range(SLOTS)], axis=0
        ).astype(BF)
        tokens = jnp.concatenate([xq[q, s, 0:TOK, :] for q in range(4)], axis=1)
        packed = jnp.dot(chosen, tokens, preferred_element_type=F32).astype(BF)
        for j in range(SLOTS):
            xc[j, pl.ds(pl.multiple_of(s * CAP, 16), CAP), :] = packed[j * CAP : (j + 1) * CAP, :]
        return carry

    def compact_some(count, where):
        lax.fori_loop(0, count, functools.partial(compact, where), 0)

    ready = {
        8: ((1, lambda h, m: (h, m)),),
        24: ((4, lambda h, m: ((1 - h) * (1 + 2 * m), h * (1 + 2 * m))),),
        44: ((2, lambda h, m: (2 * m, 2 - 2 * m)), (4, lambda h, m: (1 + 2 * h, 1 + 2 * m))),
        58: ((4, lambda h, m: ((1 - h) * (1 + 2 * m) + 2 * h, h * (1 + 2 * m) + 2 - 2 * h)),),
    }
    for n, (_, _, run) in enumerate(events):
        pump(22.5 + 0.38 * n)
        run()
        for group in ready.get(n, ()):
            compact_some(*group)
    pump(45)
    compact_some(1, lambda h, m: (2 + h, 2 + m))
    pump(53)

    def gate_up(c, n, carry):
        j = lax.div(n, 2)
        at = pl.ds(pl.multiple_of(lax.rem(n, 2) * 384, 128), 384)
        both = jnp.dot(xc[j, at, :], wgu[c, j], preferred_element_type=F32)
        g, u = both[:, 0:HALF], both[:, HALF:]
        act[j, at, c * HALF : (c + 1) * HALF] = (g / (1.0 + jnp.exp(-g)) * u).astype(BF)
        return carry

    pump(54)
    for r in gu[0]:
        r.from_partner()
    for g in range(2):
        lax.fori_loop(g * 4, g * 4 + 4, functools.partial(gate_up, 0), 0)
        pump((57, 60)[g])
    for r in gu[1]:
        r.from_partner()
    for g in range(2):
        lax.fori_loop(g * 4, g * 4 + 4, functools.partial(gate_up, 1), 0)
        pump(62)

    def down(h, j, carry):
        out = jnp.dot(act[j], wd[h, j], preferred_element_type=F32)
        yc[j, :, h * HW : (h + 1) * HW] = out.astype(BF)
        return carry

    def combine(h, s, carry):
        at = pl.ds(pl.multiple_of(s * CAP, 16), CAP)
        outs = jnp.concatenate([yc[j, at, h * HW : (h + 1) * HW] for j in range(SLOTS)], axis=0)
        total = lax.dot_general(pw[s], outs, TN, preferred_element_type=F32).astype(BF)
        for i in range(2):
            part[2 * h + i, s] = total[:, i * QW : (i + 1) * QW]
        return carry

    def ahead(v, h, dirn, k):
        left = h - k
        return wrap(v + left, 4) if dirn == 0 else wrap(v - left, 4)

    def s1_go(q, o, dirn, k):
        a, b, na, nb = axes(q)
        i = hop_index(q, dirn, k)
        target = cid(q, ahead(a, PHOPS[q][dirn], dirn, k), wrap(b + o, 4))
        send(part.at[q, target], rb1.at[q, i, o], r1_s.at[q, i, o], r1_r.at[q, i, o], na[dirn])

    def s2_go(q, dirn, k):
        a, b, na, nb = axes(q)
        i = hop_index(q, dirn, k)
        target = cid(q, a, ahead(b, PHOPS[q][dirn], dirn, k))
        send(part.at[q, target], rb2.at[q, i], r2_s.at[q, i], r2_r.at[q, i], nb[dirn])

    def s1_wait(q, o, dirn, k):
        i = hop_index(q, dirn, k)
        arrived(rb1.at[q, i, o], r1_s.at[q, i, o], r1_r.at[q, i, o])
        return rb1[q, i, o].astype(F32)

    def s2_wait(q, dirn, k):
        i = hop_index(q, dirn, k)
        arrived(rb2.at[q, i], r2_s.at[q, i], r2_r.at[q, i])
        return rb2[q, i].astype(F32)

    def add_into(q, idx, *terms):
        total = part[q, idx].astype(F32)
        for t in terms:
            total = total + t
        part[q, idx] = total.astype(BF)

    offsets = (2, 1, 3, 0)
    own = [None] * 4

    def s1_first(h):
        for o in offsets:
            for q in (2 * h, 2 * h + 1):
                for dirn in range(2):
                    s1_go(q, o, dirn, 0)

    def s1_far(h):
        for o in offsets:
            for q in (2 * h, 2 * h + 1):
                a, b, na, nb = axes(q)
                far = 0 if PHOPS[q][0] == 2 else 1
                add_into(q, cid(q, ahead(a, 2, far, 1), wrap(b + o, 4)), s1_wait(q, o, far, 0))
                s1_go(q, o, far, 1)

    def s1_end(h):
        for o in offsets:
            for q in (2 * h, 2 * h + 1):
                a, b, na, nb = axes(q)
                right, left = PHOPS[q]
                terms = [s1_wait(q, o, 0, right - 1), s1_wait(q, o, 1, left - 1)]
                far = 0 if right == 2 else 1
                mid = 1 if far == 0 else 3
                add_into(q, cid(q, a, wrap(b + o, 4)), *terms)
                if o == 2:
                    s2_go(q, far, 0)
                elif o == 4 - mid:
                    s2_go(q, 1 - far, 0)

    def s2_far(h):
        for q in (2 * h, 2 * h + 1):
            a, b, na, nb = axes(q)
            far = 0 if PHOPS[q][0] == 2 else 1
            add_into(q, cid(q, a, ahead(b, 2, far, 1)), s2_wait(q, far, 0))
            s2_go(q, far, 1)

    def s2_end(h):
        for q in (2 * h, 2 * h + 1):
            right, left = PHOPS[q]
            own[q] = part[q, chip].astype(F32) + s2_wait(q, 0, right - 1) + s2_wait(q, 1, left - 1)

    def produce(h):
        for r in dn[h]:
            r.from_partner()
        lax.fori_loop(0, SLOTS, functools.partial(down, h), 0)
        pump(64)
        lax.fori_loop(0, CHIPS, functools.partial(combine, h), 0, unroll=4)
        s1_first(h)
        pump(68)

    produce(0)
    produce(1)
    s1_far(0)
    s1_far(1)
    s1_end(0)
    s2_far(0)
    s1_end(1)
    s2_far(1)
    s2_end(0)
    s2_end(1)
    mixture = jnp.concatenate(own, axis=1)
    out_ref[...] = rms(hid[...].astype(F32) + mixture, fgain[...]).astype(BF)

    for copy in sends:
        copy.wait_send()


def body(
    head_outputs,
    residual,
    output_weight,
    router,
    norm_gain,
    placed_gate_up,
    placed_down,
    routes,
    replica_pick,
    placement,
    final_gain,
):
    dma = pltpu.SemaphoreType.DMA
    anywhere = pl.BlockSpec(memory_space=pl.ANY)
    vmem = pl.BlockSpec(memory_space=pltpu.VMEM)
    return pl.pallas_call(
        body_kernel,
        out_shape=jax.ShapeDtypeStruct((TOK, D), BF),
        in_specs=[anywhere] * 5 + [vmem] * 6,
        out_specs=vmem,
        scratch_shapes=[
            pltpu.VMEM((TOK, D), BF),
            pltpu.VMEM((TOK, D), BF),
            pltpu.VMEM((4, D, QW), BF),
            pltpu.VMEM((2, SLOTS, D, FF), BF),
            pltpu.VMEM((2, SLOTS, FF, HW), BF),
            pltpu.VMEM((4, CHIPS, TOK + 32, QW), BF),
            pltpu.VMEM((SLOTS, ROWS, D), BF),
            pltpu.VMEM((SLOTS, ROWS, FF), BF),
            pltpu.VMEM((SLOTS, ROWS, D), BF),
            pltpu.VMEM((4, CHIPS, TOK, QW), BF),
            pltpu.VMEM((4, 3, 4, TOK, QW), BF),
            pltpu.VMEM((4, 3, TOK, QW), BF),
            pltpu.VMEM((TOK, D), BF),
            pltpu.VMEM((CHIPS, SLOTS * CAP, TOK), BF),
            dma((18,)),
            dma((2, 8)),
            dma((2, 8)),
            dma((2, 8)),
            dma((2, 8)),
            dma((8, 8)),
            dma((8, 8)),
            dma((8, 9)),
            dma((8, 9)),
            dma((4, 3)),
            dma((4, 3)),
            dma((4, 4, 3)),
            dma((4, 4, 3)),
            dma((4, 3, 4)),
            dma((4, 3, 4)),
            dma((4, 3)),
            dma((4, 3)),
        ],
        compiler_params=pltpu.CompilerParams(
            collective_id=0, has_side_effects=True, vmem_limit_bytes=60 * 1024 * 1024
        ),
    )(
        head_outputs,
        residual,
        output_weight,
        placed_gate_up,
        placed_down,
        router.T,
        norm_gain.reshape(1, D),
        final_gain.reshape(1, D),
        routes.T,
        replica_pick.T,
        placement.reshape(1, PL),
    )


def solution(mesh):
    return jax.shard_map(
        body,
        mesh=mesh,
        in_specs=(
            P(("expert", "shard"), None),
            P(("expert", "shard"), None),
            P("shard", None),
            P(),
            P(),
            P("expert", "shard", None),
            P("expert", "shard", None),
            P(("expert", "shard"), None),
            P(("expert", "shard"), None),
            P(),
            P(),
        ),
        out_specs=P(("expert", "shard"), None),
        check_vma=False,
    )
```
